256 devices in a mesh: row: 16 (over z_hi, x, core), col: 16 (over z_lo, y).
Axes of the slice: x: 4, y: 4, z: 8 (z_hi: 2, z_lo: 4; z = z_hi * 4 + z_lo), core: 2. Of those that a mesh axis runs over, the one named last changes fastest.
Arguments:
- ao_ints: bfloat16 [5120, 15360], P(('row', 'col')), may hold values from -6 to 6
- vir_coef: bfloat16 [5120, 128], P(('row', 'col')), may hold values from -0.3125 to 0.3125
- naf_vectors: bfloat16 [15360, 7168], P('row', 'col'), may hold values from -0.046875 to 0.046875
Outputs:
- gram: float32 [15360, 15360], P('row', 'col')
- naf_ints: float32 [128, 7168], P('row', 'col')
The draws below stay inside these ranges and needn't reach their ends.
All inputs are finite; a program needn't handle non-finite values.
Results may differ from the reference program's by a relative error of at most 0.004.
Values may be sent and summed in bfloat16 or wider, within the bound.
A program may use at most 64 MiB of HBM per device.

```python
import jax
import jax.numpy as jnp

NAO = 5120
NAUX = 15360
NNAF = 7168
VB = 128


def with_spikes(entries, stream_key, source, target, shards_of, factor):
    def block_of(dim):
        return (jnp.arange(entries.shape[dim]) // (entries.shape[dim] // shards_of)).reshape((-1,) + (1,) * (entries.ndim - 1 - dim))

    first = jax.random.permutation(stream_key, shards_of)[block_of(target)]
    other_side = (block_of(target) + shards_of // 2) % shards_of
    return jnp.where((block_of(source) == first) | (block_of(source) == other_side), factor * entries, entries)


def block_scale(stream_key, shape, split, low, largest):
    def one(position, shards_of):
        steps = jax.random.uniform(jax.random.fold_in(jax.random.fold_in(stream_key, 6), position), (shards_of,), jnp.float32, low / len(split), largest / len(split))
        return jnp.repeat(jnp.exp(steps), shape[position] // shards_of).reshape((-1,) + (1,) * (len(shape) - position - 1))

    loudness = one(*split[0])
    for cut in split[1:]:
        loudness = loudness * one(*cut)
    return loudness


def bell_draw(stream_key, dims, width, most, cuts=(), held_as=jnp.bfloat16):
    level = block_scale(stream_key, dims, cuts, -0.22, 0.18) if cuts else 1.0
    result = jax.random.normal(stream_key, dims, jnp.float32) * width * level
    return jnp.minimum(jnp.maximum(result, -most), most).astype(held_as)


def heavy_noise(key, shape, width, most, split, heavy, dtype=jnp.bfloat16):
    values = width * jax.random.normal(key, shape, jnp.float32)
    if split:
        values = values * block_scale(key, shape, split, -0.22, 0.18)
    return jnp.clip(with_spikes(values, jax.random.fold_in(key, 3), *heavy), -most, most).astype(dtype)


def setup_inputs(seed: int = 0) -> dict:
    streams_of = jax.random.split(jax.random.key(seed), 4)
    return {
        "ao_ints": bell_draw(streams_of[0], (NAO, NAUX), 1.0, 6.0, ((0, 256),)),
        "vir_coef": heavy_noise(streams_of[1], (NAO, VB), NAO ** -0.5, 0.3125, ((0, 256),), (0, 1, 128, 5.5)),
        "naf_vectors": bell_draw(streams_of[2], (NAUX, NNAF), NAUX ** -0.5, 0.046875, ((0, 16), (1, 16))),
    }


def reference(ao_ints, vir_coef, naf_vectors):
    half = jnp.dot(vir_coef.T, ao_ints, preferred_element_type=jnp.float32)
    bia = half.astype(jnp.bfloat16)
    gram = jnp.dot(bia.T, bia, preferred_element_type=jnp.float32) * (1.0 / VB)
    naf_ints = jnp.dot(bia, naf_vectors, preferred_element_type=jnp.float32)
    return gram, naf_ints
```

```python
import jax
import jax.numpy as jnp
from jax import lax
from jax.experimental import pallas as pl
from jax.experimental.pallas import tpu as pltpu
from jax.sharding import PartitionSpec as P

MESH = pl.DeviceIdType.MESH
F32 = jnp.float32
BF16 = jnp.bfloat16

LINE = 8
PLANE = 32
OWNERS = 30
UNIT = 64
PANEL = 15


def contract_first(lhs, rhs):
    return lax.dot_general(lhs, rhs, (((0,), (0,)), ((), ())), preferred_element_type=F32)


def contract_second(lhs, rhs):
    return lax.dot_general(lhs, rhs, (((1,), (1,)), ((), ())), preferred_element_type=F32)


def kernel(
    ao_hbm, vir_ref, naf_hbm, gram_ref, naf_ref,
    ao, naf, stage, raw, part, terms, units, rowp, colp, proj, projs,
    load_sem, raw_send, raw_recv, term_send, term_recv, unit_send, unit_recv,
    row_send, col_send, row_recv, col_recv, proj_send, proj_recv,
):
    r = lax.axis_index("row")
    c = lax.axis_index("col")
    zh, i, zl, y = r // 8, r % 8, c // 4, c % 4
    z = 4 * zh + zl
    base = (15 * y + 1) // 2
    owner = base + i
    owns = i < 8 - y % 2

    def term_copy(other):
        return pltpu.make_async_remote_copy(
            src_ref=part.at[other], dst_ref=terms.at[z],
            send_sem=term_send.at[other], recv_sem=term_recv,
            device_id=(8 * (other // 4) + i, 4 * (other % 4) + y), device_id_type=MESH,
        )

    def unit_copy(step):
        if step < 3:
            to_zh, to_zl = zh, (zl + step + 1) % 4
        else:
            to_zh, to_zl = 1 - zh, z // 2
        return pltpu.make_async_remote_copy(
            src_ref=units.at[z], dst_ref=units.at[z],
            send_sem=unit_send.at[step], recv_sem=unit_recv,
            device_id=(8 * to_zh + i, 4 * to_zl + y), device_id_type=MESH,
        )

    def row_target(step):
        unit = 4 * zh + step // 4
        place = 2 * owner + unit % 2
        return unit, 4 * (unit // 2) + place // 15, place % 15, 4 * zl + (y + step) % 4

    def row_copy(step):
        unit, panel, slot, col = row_target(step)
        return pltpu.make_async_remote_copy(
            src_ref=units.at[unit], dst_ref=rowp.at[slot],
            send_sem=row_send.at[step], recv_sem=row_recv,
            device_id=(panel, col), device_id_type=MESH,
        )

    def col_target(step):
        unit = 2 * zl + step // 8
        place = 2 * owner + unit % 2
        return unit, 4 * zl + place // 15, place % 15, 8 * zh + (i + step) % 8

    def col_copy(step):
        unit, panel, slot, row = col_target(step)
        return pltpu.make_async_remote_copy(
            src_ref=units.at[unit], dst_ref=colp.at[slot],
            send_sem=col_send.at[step], recv_sem=col_recv,
            device_id=(row, panel), device_id_type=MESH,
        )

    def proj_copy(other):
        return pltpu.make_async_remote_copy(
            src_ref=proj.at[other], dst_ref=projs.at[r],
            send_sem=proj_send.at[other], recv_sem=proj_recv,
            device_id=(other, c), device_id_type=MESH,
        )

    load_ao = pltpu.make_async_copy(ao_hbm, ao, load_sem.at[0])
    load_naf = pltpu.make_async_copy(naf_hbm, naf, load_sem.at[1])
    load_ao.start()
    load_naf.start()

    barrier = pltpu.get_barrier_semaphore()

    def greet(row, col):
        pl.semaphore_signal(barrier, inc=1, device_id=(row, col), device_id_type=MESH)

    @pl.loop(1, PLANE)
    def _(step):
        other = (8 * y + i + step) % PLANE
        greet(8 * zh + other % 8, 4 * zl + other // 8)

    @pl.loop(1, LINE)
    def _(step):
        other = (z + step) % LINE
        greet(8 * (other // 4) + i, 4 * (other % 4) + y)

    @pl.loop(1, 8)
    def _(step):
        greet(8 * (1 - zh) + (i + step) % 8, c)

    pl.semaphore_wait(barrier, PLANE - 1 + LINE - 1 + 7)

    load_ao.wait()
    tail = vir_ref[16:20, :].astype(F32)
    vir_tail = jnp.concatenate([tail, tail, tail, tail], axis=0).astype(BF16)
    vir_main = vir_ref[0:16, :]

    def raw_copy(dest):
        dest_y = (2 * dest) // 15
        dest_i = dest - (15 * dest_y + 1) // 2
        return pltpu.make_async_remote_copy(
            src_ref=stage.at[dest], dst_ref=raw.at[8 * y + i],
            send_sem=raw_send.at[dest], recv_sem=raw_recv,
            device_id=(8 * zh + dest_i, 4 * zl + dest_y), device_id_type=MESH,
        )

    @pl.loop(0, OWNERS)
    def _(step):
        dest = (base + i + step) % OWNERS
        tails = []
        for quarter in range(4):
            lanes = pl.ds(pl.multiple_of(128 * (30 * quarter + dest), 128), 128)
            stage[dest, 16 * quarter : 16 * quarter + 16, :] = ao[0:16, lanes]
            tails.append(ao[16:20, lanes].astype(F32))
        stage[dest, 64:80, :] = jnp.concatenate(tails, axis=0).astype(BF16)
        stage[dest, 80:96, :] = vir_main
        stage[dest, 96:112, :] = vir_tail
        mine = jnp.logical_and(owns, dest == owner)

        @pl.when(mine)
        def _():
            pltpu.make_async_copy(stage.at[dest], raw.at[8 * y + i], raw_recv).start()

        @pl.when(jnp.logical_not(mine))
        def _():
            raw_copy(dest).start()

    @pl.when(owns)
    def _():
        pltpu.make_async_copy(raw, raw, raw_recv).wait()
        coeff = raw[:, 80:96, :].reshape(512, 128)
        coeff_tail = raw[:, 96:112, :].reshape(512, 128)
        ints_tail = raw[:, 64:80, :].reshape(512, 128)
        which = (lax.broadcasted_iota(jnp.int32, (512, 128), 0) // 4) % 4
        for quarter in range(4):
            ints = raw[:, 16 * quarter : 16 * quarter + 16, :].reshape(512, 128)
            picked = jnp.where(which == quarter, coeff_tail.astype(F32), 0.0).astype(BF16)
            half = contract_first(ints, coeff) + contract_first(ints_tail, picked)
            part[2 * quarter, :, :] = half[0:UNIT, :]
            part[2 * quarter + 1, :, :] = half[UNIT:, :]

        pltpu.make_async_copy(part.at[z], terms.at[z], term_recv).start()

        @pl.loop(1, LINE)
        def _(step):
            other = (z + step) % LINE
            term_copy(other).start()

        pltpu.make_async_copy(terms, terms, term_recv).wait()
        total = terms[0, :, :]
        for s in range(1, LINE):
            total = total + terms[s, :, :]
        units[z, :, :] = total.astype(BF16)

        for step in range(4):
            unit_copy(step).start()
        crossed = zl // 2 != zh

        @pl.when(crossed)
        def _():
            pltpu.make_async_copy(units.at[pl.ds(0, 5)], units.at[pl.ds(0, 5)], unit_recv).wait()

        @pl.when(jnp.logical_not(crossed))
        def _():
            pltpu.make_async_copy(units.at[pl.ds(0, 3)], units.at[pl.ds(0, 3)], unit_recv).wait()

        @pl.loop(0, 16)
        def _(step):
            unit, panel, slot, col = row_target(step)
            mine = jnp.logical_and(panel == r, col == c)

            @pl.when(mine)
            def _():
                pltpu.make_async_copy(units.at[unit], rowp.at[slot], row_recv).start()

            @pl.when(jnp.logical_not(mine))
            def _():
                row_copy(step).start()

        @pl.loop(0, 16)
        def _(step):
            unit, panel, slot, row = col_target(step)
            mine = jnp.logical_and(panel == c, row == r)

            @pl.when(mine)
            def _():
                pltpu.make_async_copy(units.at[unit], colp.at[slot], col_recv).start()

            @pl.when(jnp.logical_not(mine))
            def _():
                col_copy(step).start()

    load_naf.wait()
    pltpu.make_async_copy(rowp, rowp, row_recv).wait()
    rows = rowp[...].reshape(PANEL * UNIT, 128)
    proj[...] = contract_first(rows, naf[...]).reshape(16, 8, naf.shape[1])
    pltpu.make_async_copy(proj.at[r], projs.at[r], proj_recv).start()

    @pl.loop(1, 16)
    def _(step):
        proj_copy((r + step) % 16).start()

    pltpu.make_async_copy(colp, colp, col_recv).wait()
    cols = colp[...].reshape(PANEL * UNIT, 128)
    for part_of in range(5):
        block = rowp[3 * part_of : 3 * part_of + 3, :, :].reshape(3 * UNIT, 128)
        gram_ref[3 * UNIT * part_of : 3 * UNIT * (part_of + 1), :] = contract_second(block, cols) * (1.0 / 128)

    pltpu.make_async_copy(projs, projs, proj_recv).wait()
    total = projs[0, :, :]
    for s in range(1, 16):
        total = total + projs[s, :, :]
    naf_ref[...] = total

    @pl.loop(0, OWNERS)
    def _(dest):
        @pl.when(jnp.logical_not(jnp.logical_and(owns, dest == owner)))
        def _():
            raw_copy(dest).wait_send()

    @pl.when(owns)
    def _():
        @pl.loop(1, LINE)
        def _(step):
            term_copy((z + step) % LINE).wait_send()

        for step in range(4):
            unit_copy(step).wait_send()

        @pl.loop(0, 16)
        def _(step):
            unit, panel, slot, col = row_target(step)

            @pl.when(jnp.logical_not(jnp.logical_and(panel == r, col == c)))
            def _():
                row_copy(step).wait_send()

        @pl.loop(0, 16)
        def _(step):
            unit, panel, slot, row = col_target(step)

            @pl.when(jnp.logical_not(jnp.logical_and(panel == c, row == r)))
            def _():
                col_copy(step).wait_send()

    @pl.loop(1, 16)
    def _(step):
        proj_copy((r + step) % 16).wait_send()


def shards(ao_ints, vir_coef, naf_vectors):
    dma = pltpu.SemaphoreType.DMA
    return pl.pallas_call(
        kernel,
        out_shape=(
            jax.ShapeDtypeStruct((960, 960), F32),
            jax.ShapeDtypeStruct((8, 448), F32),
        ),
        in_specs=[
            pl.BlockSpec(memory_space=pl.ANY),
            pl.BlockSpec(memory_space=pltpu.VMEM),
            pl.BlockSpec(memory_space=pl.ANY),
        ],
        out_specs=(
            pl.BlockSpec(memory_space=pltpu.VMEM),
            pl.BlockSpec(memory_space=pltpu.VMEM),
        ),
        scratch_shapes=[
            pltpu.VMEM((20, 15360), BF16),
            pltpu.VMEM((960, 448), BF16),
            pltpu.VMEM((OWNERS, 112, 128), BF16),
            pltpu.VMEM((PLANE, 112, 128), BF16),
            pltpu.VMEM((LINE, UNIT, 128), F32),
            pltpu.VMEM((LINE, UNIT, 128), F32),
            pltpu.VMEM((LINE, UNIT, 128), BF16),
            pltpu.VMEM((PANEL, UNIT, 128), BF16),
            pltpu.VMEM((PANEL, UNIT, 128), BF16),
            pltpu.VMEM((16, 8, 448), F32),
            pltpu.VMEM((16, 8, 448), F32),
            dma((2,)), dma((OWNERS,)), dma, dma((LINE,)), dma, dma((4,)), dma,
            dma((16,)), dma((16,)), dma, dma, dma((16,)), dma,
        ],
        compiler_params=pltpu.CompilerParams(
            collective_id=0, has_side_effects=True, vmem_limit_bytes=40 * 1024 * 1024
        ),
        name="gram_and_projection",
    )(ao_ints, vir_coef, naf_vectors)


def solution(mesh):
    in_specs = (P(("row", "col"), None), P(("row", "col"), None), P("row", "col"))
    out_specs = (P("row", "col"), P("row", "col"))
    return jax.shard_map(shards, mesh=mesh, in_specs=in_specs, out_specs=out_specs, check_vma=False)
```

```python
import jax
import jax.numpy as jnp
from jax import lax
from jax.experimental import pallas as pl
from jax.experimental.pallas import tpu as pltpu
from jax.sharding import PartitionSpec as P

MESH = pl.DeviceIdType.MESH
F32 = jnp.float32
BF16 = jnp.bfloat16

LINE = 8
PLANE = 32
UNIT = 64
PANEL = 15
SHIFTS = (2, 1, 3, 0)
SPANS = ((0, 32), (32, 48), (48, 64), (64, 80))


def contract_first(lhs, rhs):
    return lax.dot_general(lhs, rhs, (((0,), (0,)), ((), ())), preferred_element_type=F32)


def contract_second(lhs, rhs):
    return lax.dot_general(lhs, rhs, (((1,), (1,)), ((), ())), preferred_element_type=F32)


def owner_of(x, y, core):
    return (15 * y + 1) // 2 + 2 * x + core, 2 * x + core < 8 - y % 2


def kernel(
    ao_hbm, vir_hbm, naf_hbm, gram_ref, naf_ref,
    ao, vir, naf, stage, raw, vsend, coeffs, part, terms, units, rowp, colp, proj, projs,
    load_sem, vir_send, vir_recv, pass_send, pass_recv, raw_send, raw_recv, self_sem, term_send, term_recv,
    unit_send, unit_recv, row_send, col_send, row_recv, col_recv, proj_send, proj_recv,
):
    r = lax.axis_index("row")
    c = lax.axis_index("col")
    zh, x, core, zl, y = r // 8, (r // 2) % 4, r % 2, c // 4, c % 4
    i = 2 * x + core
    z = 4 * zh + zl
    chip = 4 * y + x
    place = 16 * core + chip
    owner, owns = owner_of(x, y, core)

    load_ao = pltpu.make_async_copy(ao_hbm, ao, load_sem.at[0])
    load_naf = pltpu.make_async_copy(naf_hbm, naf, load_sem.at[1])
    load_vir = pltpu.make_async_copy(vir_hbm, vir, load_sem.at[2])
    load_vir.start()
    load_ao.start()
    load_naf.start()

    barrier = pltpu.get_barrier_semaphore()

    def greet(row, col):
        pl.semaphore_signal(barrier, inc=1, device_id=(row, col), device_id_type=MESH)

    def in_plane(where):
        return 8 * zh + 2 * (where % 4) + where // 16, 4 * zl + (where // 4) % 4

    def in_line(where):
        return 8 * (where // 4) + i, 4 * (where % 4) + y

    @pl.loop(1, PLANE)
    def _(step):
        greet(*in_plane((place + step) % PLANE))

    @pl.loop(1, LINE)
    def _(step):
        greet(*in_line((z + step) % LINE))

    @pl.loop(1, 8)
    def _(step):
        greet(8 * (1 - zh) + (i + step) % 8, c)

    def vir_copy(other):
        return pltpu.make_async_remote_copy(
            src_ref=vsend, dst_ref=coeffs.at[core, chip],
            send_sem=vir_send, recv_sem=vir_recv,
            device_id=in_plane(16 * core + other), device_id_type=MESH,
        )

    pass_copy = pltpu.make_async_remote_copy(
        src_ref=coeffs.at[core], dst_ref=coeffs.at[core],
        send_sem=pass_send, recv_sem=pass_recv,
        device_id=(r + 1 - 2 * core, c), device_id_type=MESH,
    )

    def raw_copy(dest, turn):
        first, last = SPANS[turn]
        return pltpu.make_async_remote_copy(
            src_ref=stage.at[dest, first:last], dst_ref=raw.at[place, first:last],
            send_sem=raw_send.at[turn], recv_sem=raw_recv.at[turn],
            device_id=in_plane(dest), device_id_type=MESH,
        )

    def term_copy(other, turn):
        return pltpu.make_async_remote_copy(
            src_ref=part.at[other], dst_ref=terms.at[z],
            send_sem=term_send, recv_sem=term_recv,
            device_id=in_line(other), device_id_type=MESH,
        )

    def unit_copy(step):
        if step < 3:
            other = 4 * zh + (zl + step + 1) % 4
        else:
            other = 4 * (1 - zh) + z // 2
        return pltpu.make_async_remote_copy(
            src_ref=units.at[z], dst_ref=units.at[z],
            send_sem=unit_send.at[step], recv_sem=unit_recv.at[z],
            device_id=in_line(other), device_id_type=MESH,
        )

    def await_unit(unit):
        pltpu.make_async_copy(units.at[unit], units.at[unit], unit_recv.at[unit]).wait()

    def row_target(step):
        unit = 4 * zh + (zl + step // 4) % 4
        spot = 2 * owner + unit % 2
        return unit, 4 * (unit // 2) + spot // 15, spot % 15, 4 * zl + (y + step) % 4

    def row_copy(step):
        unit, panel, slot, col = row_target(step)
        return pltpu.make_async_remote_copy(
            src_ref=units.at[unit], dst_ref=rowp.at[slot],
            send_sem=row_send.at[step], recv_sem=row_recv,
            device_id=(panel, col), device_id_type=MESH,
        )

    def row_here(step):
        unit, panel, slot, col = row_target(step)
        return jnp.logical_and(panel == r, col == c)

    def col_target(step):
        unit = 2 * zl + step // 8
        spot = 2 * owner + unit % 2
        return unit, 4 * zl + spot // 15, spot % 15, 8 * zh + (i + step) % 8

    def col_copy(step):
        unit, panel, slot, row = col_target(step)
        return pltpu.make_async_remote_copy(
            src_ref=units.at[unit], dst_ref=colp.at[slot],
            send_sem=col_send.at[step], recv_sem=col_recv,
            device_id=(row, panel), device_id_type=MESH,
        )

    def col_here(step):
        unit, panel, slot, row = col_target(step)
        return jnp.logical_and(panel == c, row == r)

    def proj_copy(other):
        return pltpu.make_async_remote_copy(
            src_ref=proj.at[other], dst_ref=projs.at[r],
            send_sem=proj_send, recv_sem=proj_recv,
            device_id=(other, c), device_id_type=MESH,
        )

    def wait_bytes(ref, sem):
        pltpu.make_async_copy(ref, ref, sem).wait()

    load_vir.wait()
    tail = vir[16:20, :].astype(F32)
    vsend[0:16, :] = vir[0:16, :]
    vsend[16:32, :] = jnp.concatenate([tail, tail, tail, tail], axis=0).astype(BF16)
    coeffs[core, chip, :, :] = vsend[...]
    load_ao.wait()
    turns = []
    for quarter in range(4):
        ahead = (quarter + 4 - z // 2) % 4
        turns.append(jnp.where(ahead == 0, 3, jnp.where(ahead == 1, 1, jnp.where(ahead == 2, 0, 2))))
    for dest in range(PLANE):
        theirs, has = owner_of(dest % 4, (dest // 4) % 4, dest // 16)
        if not has:
            continue
        tails = []
        for quarter in range(4):
            lanes = slice(128 * (30 * quarter + theirs), 128 * (30 * quarter + theirs) + 128)
            stage[dest, pl.ds(pl.multiple_of(16 + 16 * turns[quarter], 16), 16), :] = ao[0:16, lanes]
            tails.append(ao[16:20, lanes].astype(F32))
        stage[dest, 0:16, :] = jnp.concatenate(tails, axis=0).astype(BF16)

    pl.semaphore_wait(barrier, PLANE - 1 + LINE - 1 + 7)

    @pl.loop(1, 16)
    def _(step):
        vir_copy((chip + 7 * step) % 16).start()

    for turn in range(4):
        first, last = SPANS[turn]

        @pl.when(owns)
        def _():
            pltpu.make_async_copy(stage.at[place, first:last], raw.at[place, first:last], self_sem.at[turn]).start()

        @pl.loop(1, PLANE)
        def _(step):
            dest = (place + 7 * step) % PLANE
            _, has = owner_of(dest % 4, (dest // 4) % 4, dest // 16)

            @pl.when(has)
            def _():
                raw_copy(dest, turn).start()

    wait_bytes(coeffs.at[core, pl.ds(0, 15)], vir_recv)
    pass_copy.start()
    pass_copy.wait_recv()

    @pl.when(owns)
    def _():
        coeff = coeffs[:, :, 0:16, :].reshape(512, 128)
        coeff_tail = coeffs[:, :, 16:32, :].reshape(512, 128).astype(F32)
        which = (lax.broadcasted_iota(jnp.int32, (512, 128), 0) // 4) % 4
        for turn in range(4):
            quarter = (z // 2 + SHIFTS[turn]) % 4
            first, last = SPANS[turn]
            wait_bytes(raw.at[place, first:last], self_sem.at[turn])
            wait_bytes(raw.at[pl.ds(0, PLANE - 1), first:last], raw_recv.at[turn])
            ints = raw[:, last - 16 : last, :].reshape(512, 128)
            ints_tail = raw[:, 0:16, :].reshape(512, 128)
            picked = jnp.where(which == quarter, coeff_tail, 0.0).astype(BF16)
            half = contract_first(ints, coeff) + contract_first(ints_tail, picked)
            for unit in range(2):
                part[2 * quarter + unit, :, :] = half[UNIT * unit : UNIT * (unit + 1), :]
                other = 2 * quarter + unit
                if turn < 3:
                    term_copy(other, turn).start()
                else:

                    @pl.when(other != z)
                    def _():
                        term_copy(other, turn).start()

        terms[z, :, :] = part[z, :, :]
        wait_bytes(terms.at[pl.ds(0, LINE - 1)], term_recv)
        total = terms[0, :, :]
        for s in range(1, LINE):
            total = total + terms[s, :, :]
        units[z, :, :] = total.astype(BF16)

        for step in range(4):
            unit_copy(step).start()
        for ahead in range(4):
            if ahead:
                await_unit(4 * zh + (zl + ahead) % 4)

            @pl.loop(4 * ahead, 4 * ahead + 4)
            def _(step):
                unit, panel, slot, col = row_target(step)
                here = row_here(step)

                @pl.when(here)
                def _():
                    pltpu.make_async_copy(units.at[unit], rowp.at[slot], row_recv).start()

                @pl.when(jnp.logical_not(here))
                def _():
                    row_copy(step).start()

    load_naf.wait()
    wait_bytes(rowp, row_recv)
    rows = rowp[...].reshape(PANEL * UNIT, 128)
    share = lax.dot_general(naf[...], rows, (((1,), (0,)), ((), ())), preferred_element_type=F32)
    proj[...] = share.T.reshape(16, 8, naf.shape[0])

    @pl.loop(1, 16)
    def _(step):
        proj_copy((r + step) % 16).start()

    projs[r, :, :] = proj[r, :, :]

    @pl.when(owns)
    def _():
        @pl.when(zl // 2 != zh)
        def _():
            await_unit(2 * zl)
            await_unit(2 * zl + 1)

        @pl.loop(0, 16)
        def _(step):
            unit, panel, slot, row = col_target(step)
            here = col_here(step)

            @pl.when(here)
            def _():
                pltpu.make_async_copy(units.at[unit], colp.at[slot], col_recv).start()

            @pl.when(jnp.logical_not(here))
            def _():
                col_copy(step).start()

    wait_bytes(colp, col_recv)
    cols = colp[...].reshape(PANEL * UNIT, 128)
    for band in range(5):
        block = rowp[3 * band : 3 * band + 3, :, :].reshape(3 * UNIT, 128)
        gram_ref[3 * UNIT * band : 3 * UNIT * (band + 1), :] = contract_second(block, cols) * (1.0 / 128)

    wait_bytes(projs.at[pl.ds(0, 15)], proj_recv)
    total = projs[0, :, :]
    for s in range(1, 16):
        total = total + projs[s, :, :]
    naf_ref[...] = total

    wait_bytes(coeffs.at[core, pl.ds(0, 15)], vir_send)
    pass_copy.wait_send()
    for turn in range(4):
        first, last = SPANS[turn]

        @pl.when(owns)
        def _():
            wait_bytes(stage.at[pl.ds(0, 29), first:last], raw_send.at[turn])

        @pl.when(jnp.logical_not(owns))
        def _():
            wait_bytes(stage.at[pl.ds(0, 30), first:last], raw_send.at[turn])

    @pl.when(owns)
    def _():
        wait_bytes(part.at[pl.ds(0, LINE - 1)], term_send)
        for step in range(4):
            unit_copy(step).wait_send()

        @pl.loop(0, 16)
        def _(step):
            @pl.when(jnp.logical_not(row_here(step)))
            def _():
                row_copy(step).wait_send()

        @pl.loop(0, 16)
        def _(step):
            @pl.when(jnp.logical_not(col_here(step)))
            def _():
                col_copy(step).wait_send()

    wait_bytes(proj.at[pl.ds(0, 15)], proj_send)


def shards(ao_ints, vir_coef, naf_vectors):
    dma = pltpu.SemaphoreType.DMA
    hbm = pl.BlockSpec(memory_space=pltpu.HBM)
    return pl.pallas_call(
        kernel,
        out_shape=(
            jax.ShapeDtypeStruct((960, 960), F32),
            jax.ShapeDtypeStruct((8, 448), F32),
        ),
        in_specs=[hbm, hbm, hbm],
        out_specs=(
            pl.BlockSpec(memory_space=pltpu.VMEM),
            pl.BlockSpec(memory_space=pltpu.VMEM),
        ),
        scratch_shapes=[
            pltpu.VMEM((20, 15360), BF16),
            pltpu.VMEM((20, 128), BF16),
            pltpu.VMEM((448, 960), BF16),
            pltpu.VMEM((PLANE, 80, 128), BF16),
            pltpu.VMEM((PLANE, 80, 128), BF16),
            pltpu.VMEM((32, 128), BF16),
            pltpu.VMEM((2, 16, 32, 128), BF16),
            pltpu.VMEM((LINE, UNIT, 128), F32),
            pltpu.VMEM((LINE, UNIT, 128), F32),
            pltpu.VMEM((LINE, UNIT, 128), BF16),
            pltpu.VMEM((PANEL, UNIT, 128), BF16),
            pltpu.VMEM((PANEL, UNIT, 128), BF16),
            pltpu.VMEM((16, 8, 448), F32),
            pltpu.VMEM((16, 8, 448), F32),
            dma((3,)), dma, dma, dma, dma, dma((4,)), dma((4,)), dma((4,)), dma, dma,
            dma((4,)), dma((LINE,)), dma((16,)), dma((16,)), dma, dma, dma, dma,
        ],
        compiler_params=pltpu.CompilerParams(
            collective_id=0, has_side_effects=True, vmem_limit_bytes=40 * 1024 * 1024
        ),
        name="gram_and_projection",
    )(*(pltpu.with_memory_space_constraint(a, pltpu.HBM) for a in (ao_ints, vir_coef, naf_vectors.T)))


def solution(mesh):
    in_specs = (P(("row", "col"), None), P(("row", "col"), None), P("row", "col"))
    out_specs = (P("row", "col"), P("row", "col"))
    return jax.shard_map(shards, mesh=mesh, in_specs=in_specs, out_specs=out_specs, check_vma=False)
```

```python
import jax
import jax.numpy as jnp
from jax import lax
from jax.experimental import pallas as pl
from jax.experimental.pallas import tpu as pltpu
from jax.sharding import PartitionSpec as P

MESH = pl.DeviceIdType.MESH
F32 = jnp.float32
BF16 = jnp.bfloat16

LINE = 8
PLANE = 32
UNIT = 64
PANEL = 15
SHIFTS = (2, 1, 3, 0)
SPANS = ((0, 48), (48, 64), (64, 80))
AWAITS = (0, None, 1, 2)


def contract_first(lhs, rhs):
    return lax.dot_general(lhs, rhs, (((0,), (0,)), ((), ())), preferred_element_type=F32)


def contract_second(lhs, rhs):
    return lax.dot_general(lhs, rhs, (((1,), (1,)), ((), ())), preferred_element_type=F32)


def kernel(
    ao_hbm, vir_hbm, naf_hbm, gram_ref, naf_ref,
    ao, vir, naf, stage, raw, vsend, coeffs, part, terms, unit, rowp, held, colp, proj, pair, sums, projs,
    load_sem, vir_send, vir_recv, pass_send, pass_recv, raw_send, raw_recv, term_send, term_recv,
    row_send, row_recv, hold_send, hold_recv, col_send, col_recv, half_send, half_recv, pair_send, pair_recv, proj_send, proj_recv,
):
    r = lax.axis_index("row")
    c = lax.axis_index("col")
    zh, x, core, zl, y = r // 8, (r // 2) % 4, r % 2, c // 4, c % 4
    i = 2 * x + core
    z = 4 * zh + zl
    chip = 4 * y + x
    place = 16 * core + chip
    spot = 4 * y + zl
    owns = spot < PANEL

    load_ao = pltpu.make_async_copy(ao_hbm, ao, load_sem.at[0])
    load_naf = pltpu.make_async_copy(naf_hbm, naf, load_sem.at[1])
    load_vir = pltpu.make_async_copy(vir_hbm, vir, load_sem.at[2])
    load_vir.start()
    load_ao.start()
    load_naf.start()

    barrier = pltpu.get_barrier_semaphore()

    def greet(row, col):
        pl.semaphore_signal(barrier, inc=1, device_id=(row, col), device_id_type=MESH)

    def in_plane(where):
        return 8 * zh + 2 * (where % 4) + where // 16, 4 * zl + (where // 4) % 4

    def in_line(where):
        return 8 * (where // 4) + i, 4 * (where % 4) + y

    @pl.loop(1, PLANE)
    def _(step):
        greet(*in_plane((place + step) % PLANE))

    @pl.loop(1, LINE)
    def _(step):
        greet(*in_line((z + step) % LINE))

    @pl.loop(1, 8)
    def _(step):
        greet(8 * (1 - zh) + (i + step) % 8, c)

    def vir_copy(other):
        return pltpu.make_async_remote_copy(
            src_ref=vsend, dst_ref=coeffs.at[core, chip],
            send_sem=vir_send, recv_sem=vir_recv,
            device_id=in_plane(16 * core + other), device_id_type=MESH,
        )

    pass_copy = pltpu.make_async_remote_copy(
        src_ref=coeffs.at[core], dst_ref=coeffs.at[core],
        send_sem=pass_send, recv_sem=pass_recv,
        device_id=(r + 1 - 2 * core, c), device_id_type=MESH,
    )

    def raw_copy(dest, turn):
        first, last = SPANS[turn]
        return pltpu.make_async_remote_copy(
            src_ref=stage.at[dest, first:last], dst_ref=raw.at[place, first:last],
            send_sem=raw_send.at[turn], recv_sem=raw_recv.at[turn],
            device_id=in_plane(dest), device_id_type=MESH,
        )

    def term_copy(other):
        return pltpu.make_async_remote_copy(
            src_ref=part.at[other], dst_ref=terms.at[z],
            send_sem=term_send, recv_sem=term_recv,
            device_id=in_line(other), device_id_type=MESH,
        )

    def row_copy(other):
        return pltpu.make_async_remote_copy(
            src_ref=unit, dst_ref=rowp.at[spot],
            send_sem=row_send, recv_sem=row_recv.at[y],
            device_id=(r, other), device_id_type=MESH,
        )

    goal = r // 4
    holds = x // 2 == zl % 2
    at_home = zl == goal
    goal_y = r % 4

    def hold_copy(half):
        return pltpu.make_async_remote_copy(
            src_ref=unit, dst_ref=held.at[zl],
            send_sem=hold_send, recv_sem=hold_recv,
            device_id=(8 * half + i, 4 * goal + y), device_id_type=MESH,
        )

    col_span = pl.ds(4 * y, 4)

    def col_here(other):
        return jnp.logical_and(other == x, jnp.logical_and(goal_y == y, core == y // 2))

    def col_copy(other):
        return pltpu.make_async_remote_copy(
            src_ref=held, dst_ref=colp.at[col_span],
            send_sem=col_send, recv_sem=col_recv,
            device_id=(8 * zh + 2 * other + y // 2, 4 * zl + goal_y), device_id_type=MESH,
        )

    half_span = pl.ds(8 * core, 8)
    half_copy = pltpu.make_async_remote_copy(
        src_ref=colp.at[half_span], dst_ref=colp.at[half_span],
        send_sem=half_send, recv_sem=half_recv,
        device_id=(r + 1 - 2 * core, c), device_id_type=MESH,
    )

    pair_copy = pltpu.make_async_remote_copy(
        src_ref=proj.at[1 - core], dst_ref=pair,
        send_sem=pair_send, recv_sem=pair_recv,
        device_id=(r + 1 - 2 * core, c), device_id_type=MESH,
    )

    def proj_copy(other):
        return pltpu.make_async_remote_copy(
            src_ref=sums.at[other], dst_ref=projs.at[4 * zh + x],
            send_sem=proj_send, recv_sem=proj_recv,
            device_id=(2 * other + core, c), device_id_type=MESH,
        )

    def wait_bytes(ref, sem):
        pltpu.make_async_copy(ref, ref, sem).wait()

    load_vir.wait()
    tail = vir[16:20, :].astype(F32)
    vsend[0:16, :] = vir[0:16, :]
    vsend[16:32, :] = jnp.concatenate([tail, tail, tail, tail], axis=0).astype(BF16)
    coeffs[core, chip, :, :] = vsend[...]
    load_ao.wait()
    turns = []
    for quarter in range(4):
        ahead = (quarter + 4 - z // 2) % 4
        turns.append(jnp.where(ahead == 0, 3, jnp.where(ahead == 1, 1, jnp.where(ahead == 2, 0, 2))))
    for dest in range(PLANE):
        tails = []
        for quarter in range(4):
            panel = 8 * (quarter // 2) + 2 * (dest % 4) + dest // 16
            start = 960 * panel + 256 * ((dest // 4) % 4) + 128 * (quarter % 2)
            if start % 128 == 0:
                tile = ao[:, start : start + 128].astype(F32)
            else:
                after = min(start + 64, 15360 - 128)
                tile = jnp.concatenate([ao[:, start : start + 64], ao[:, after : after + 64]], axis=1).astype(F32)
            stage[dest, pl.ds(pl.multiple_of(16 + 16 * turns[quarter], 16), 16), :] = tile[0:16].astype(BF16)
            tails.append(tile[16:20])
        stage[dest, 0:16, :] = jnp.concatenate(tails, axis=0).astype(BF16)
    raw[place, :, :] = stage[place, :, :]

    pl.semaphore_wait(barrier, PLANE - 1 + LINE - 1 + 7)

    @pl.loop(1, 16)
    def _(step):
        vir_copy((chip + 7 * step) % 16).start()

    for turn in range(len(SPANS)):

        @pl.loop(1, PLANE)
        def _(step):
            raw_copy((place + 7 * step) % PLANE, turn).start()

    wait_bytes(coeffs.at[core, pl.ds(0, 15)], vir_recv)
    pass_copy.start()
    pass_copy.wait_recv()

    coeff = coeffs[:, :, 0:16, :].reshape(512, 128)
    coeff_tail = coeffs[:, :, 16:32, :].reshape(512, 128).astype(F32)
    which = (lax.broadcasted_iota(jnp.int32, (512, 128), 0) // 4) % 4
    for turn in range(4):
        quarter = (z // 2 + SHIFTS[turn]) % 4
        if AWAITS[turn] is not None:
            first, last = SPANS[AWAITS[turn]]
            wait_bytes(raw.at[pl.ds(0, PLANE - 1), first:last], raw_recv.at[AWAITS[turn]])
        ints = raw[:, 16 * turn + 16 : 16 * turn + 32, :].reshape(512, 128)
        ints_tail = raw[:, 0:16, :].reshape(512, 128)
        picked = jnp.where(which == quarter, coeff_tail, 0.0).astype(BF16)
        half = contract_first(ints, coeff) + contract_first(ints_tail, picked)
        for which_half in range(2):
            other = 2 * quarter + which_half
            part[other, :, :] = half[UNIT * which_half : UNIT * (which_half + 1), :]
            if turn < 3:
                term_copy(other).start()
            else:

                @pl.when(other != z)
                def _():
                    term_copy(other).start()

    terms[z, :, :] = part[z, :, :]
    wait_bytes(terms.at[pl.ds(0, LINE - 1)], term_recv)
    total = terms[0, :, :]
    for s in range(1, LINE):
        total = total + terms[s, :, :]
    unit[...] = total.astype(BF16)

    @pl.when(owns)
    def _():
        pltpu.make_async_copy(unit, rowp.at[spot], row_recv.at[y]).start()

        @pl.loop(1, 16)
        def _(step):
            row_copy((c + 7 * step) % 16).start()

    for half in range(2):

        @pl.when(jnp.logical_and(at_home, zh == half))
        def _():
            pltpu.make_async_copy(unit, held.at[zl], hold_recv).start()

        @pl.when(jnp.logical_not(jnp.logical_and(at_home, zh == half)))
        def _():
            hold_copy(half).start()

    @pl.when(holds)
    def _():
        wait_bytes(held, hold_recv)

        @pl.loop(0, 4)
        def _(step):
            other = (x + step) % 4

            @pl.when(col_here(other))
            def _():
                pltpu.make_async_copy(held, colp.at[col_span], col_recv).start()

            @pl.when(jnp.logical_not(col_here(other)))
            def _():
                col_copy(other).start()

    load_naf.wait()
    share = jnp.zeros((naf.shape[0], 128), F32)
    for group in range(4):
        have = slice(4 * group, min(4 * group + 4, PANEL))
        wait_bytes(rowp.at[have], row_recv.at[group])
        rows = rowp[have, :, :].reshape(-1, 128)
        cols = naf[:, UNIT * have.start : UNIT * have.stop]
        share = share + lax.dot_general(cols, rows, (((1,), (0,)), ((), ())), preferred_element_type=F32)
    share = share.T
    for other in range(16):
        proj[other % 2, other // 2, :, :] = share[8 * other : 8 * other + 8, :]
    pair_copy.start()
    pair_copy.wait_recv()
    sums[...] = proj[core] + pair[...]

    @pl.loop(1, 8)
    def _(step):
        proj_copy((4 * zh + x + step) % 8).start()

    projs[4 * zh + x, :, :] = sums[4 * zh + x, :, :]

    wait_bytes(colp.at[half_span], col_recv)
    half_copy.start()
    half_copy.wait_recv()
    cols = colp[0:PANEL, :, :].reshape(PANEL * UNIT, 128)
    for band in range(5):
        block = rowp[3 * band : 3 * band + 3, :, :].reshape(3 * UNIT, 128)
        gram_ref[3 * UNIT * band : 3 * UNIT * (band + 1), :] = contract_second(block, cols) * (1.0 / 128)

    wait_bytes(projs.at[pl.ds(0, 7)], proj_recv)
    total = projs[0, :, :]
    for s in range(1, 8):
        total = total + projs[s, :, :]
    naf_ref[...] = total

    wait_bytes(coeffs.at[core, pl.ds(0, 15)], vir_send)
    pass_copy.wait_send()
    for turn in range(len(SPANS)):
        first, last = SPANS[turn]
        wait_bytes(stage.at[pl.ds(0, PLANE - 1), first:last], raw_send.at[turn])
    wait_bytes(part.at[pl.ds(0, LINE - 1)], term_send)

    @pl.when(owns)
    def _():
        wait_bytes(rowp, row_send)

    for count in range(1, 3):

        @pl.when(jnp.where(at_home, 1, 2) == count)
        def _():
            wait_bytes(held.at[0:count], hold_send)

    for count in range(3, 5):

        @pl.when(jnp.logical_and(holds, jnp.where(col_here(x), 3, 4) == count))
        def _():
            wait_bytes(terms.at[0 : 2 * count], col_send)

    half_copy.wait_send()
    pair_copy.wait_send()
    wait_bytes(sums.at[pl.ds(0, 7)], proj_send)


BANDS = 8


def spill(gram_ref, naf_ref, gram_hbm, naf_hbm, sems):
    rows = gram_ref.shape[0] // BANDS
    copies = [pltpu.make_async_copy(naf_ref, naf_hbm, sems.at[BANDS])]
    for band in range(BANDS):
        span = pl.ds(rows * band, rows)
        copies.append(pltpu.make_async_copy(gram_ref.at[span], gram_hbm.at[span], sems.at[band]))
    for copy in copies:
        copy.start()
    for copy in copies:
        copy.wait()


def shards(ao_ints, vir_coef, naf_vectors):
    dma = pltpu.SemaphoreType.DMA
    hbm = pl.BlockSpec(memory_space=pltpu.HBM)
    gram, naf_ints = pl.pallas_call(
        kernel,
        out_shape=(
            jax.ShapeDtypeStruct((960, 960), F32),
            jax.ShapeDtypeStruct((8, 448), F32),
        ),
        in_specs=[hbm, hbm, hbm],
        out_specs=(
            pl.BlockSpec(memory_space=pltpu.VMEM),
            pl.BlockSpec(memory_space=pltpu.VMEM),
        ),
        scratch_shapes=[
            pltpu.VMEM((20, 15360), BF16),
            pltpu.VMEM((20, 128), BF16),
            pltpu.VMEM((448, 960), BF16),
            pltpu.VMEM((PLANE, 80, 128), BF16),
            pltpu.VMEM((PLANE, 80, 128), BF16),
            pltpu.VMEM((32, 128), BF16),
            pltpu.VMEM((2, 16, 32, 128), BF16),
            pltpu.VMEM((LINE, UNIT, 128), F32),
            pltpu.VMEM((LINE, UNIT, 128), F32),
            pltpu.VMEM((UNIT, 128), BF16),
            pltpu.VMEM((PANEL, UNIT, 128), BF16),
            pltpu.VMEM((4, UNIT, 128), BF16),
            pltpu.VMEM((16, UNIT, 128), BF16),
            pltpu.VMEM((2, 8, 8, 448), F32),
            pltpu.VMEM((8, 8, 448), F32),
            pltpu.VMEM((8, 8, 448), F32),
            pltpu.VMEM((8, 8, 448), F32),
            dma((3,)), dma, dma, dma, dma, dma((3,)), dma((3,)), dma, dma,
            dma, dma((4,)), dma, dma, dma, dma, dma, dma, dma, dma, dma, dma,
        ],
        compiler_params=pltpu.CompilerParams(
            collective_id=0, has_side_effects=True, vmem_limit_bytes=40 * 1024 * 1024
        ),
        name="gram_and_projection",
    )(*(pltpu.with_memory_space_constraint(a, pltpu.HBM) for a in (ao_ints, vir_coef, naf_vectors.T)))
    return pl.pallas_call(
        spill,
        out_shape=(
            jax.ShapeDtypeStruct((960, 960), F32),
            jax.ShapeDtypeStruct((8, 448), F32),
        ),
        in_specs=[pl.BlockSpec(memory_space=pltpu.VMEM)] * 2,
        out_specs=(hbm, hbm),
        scratch_shapes=[dma((BANDS + 1,))],
        compiler_params=pltpu.CompilerParams(vmem_limit_bytes=16 * 1024 * 1024),
        name="spill",
    )(gram, naf_ints)


def solution(mesh):
    in_specs = (P(("row", "col"), None), P(("row", "col"), None), P("row", "col"))
    out_specs = (P("row", "col"), P("row", "col"))
    return jax.shard_map(shards, mesh=mesh, in_specs=in_specs, out_specs=out_specs, check_vma=False)
```

```python
import jax
import jax.numpy as jnp
from jax import lax
from jax.experimental import pallas as pl
from jax.experimental.pallas import tpu as pltpu
from jax.sharding import PartitionSpec as P

MESH = pl.DeviceIdType.MESH
F32 = jnp.float32
BF16 = jnp.bfloat16

LINE = 8
PLANE = 32
UNIT = 64
PANEL = 15
SHIFTS = (2, 1, 3, 0)
SPANS = ((0, 32), (32, 48), (48, 64), (64, 80))
FAR_FIRST = (2, 1, 3, 0)


def contract_first(lhs, rhs):
    return lax.dot_general(lhs, rhs, (((0,), (0,)), ((), ())), preferred_element_type=F32)


def contract_second(lhs, rhs):
    return lax.dot_general(lhs, rhs, (((1,), (1,)), ((), ())), preferred_element_type=F32)


def kernel(
    ao_hbm, vir_hbm, naf_hbm, gram_ref, naf_ref,
    ao, vir, naf, stage, raw, vsend, coeffs, part, terms, unit, rowp, held, colp, proj, pair, sums, projs,
    load_sem, vir_send, vir_recv, pass_send, pass_recv, raw_send, raw_recv, term_send, term_recv,
    row_send, row_recv, hold_send, hold_recv, col_send, col_recv, half_send, half_recv, pair_send, pair_recv, proj_send, proj_recv,
):
    r = lax.axis_index("row")
    c = lax.axis_index("col")
    zh, x, core, zl, y = r // 8, (r // 2) % 4, r % 2, c // 4, c % 4
    i = 2 * x + core
    z = 4 * zh + zl
    chip = 4 * y + x
    place = 16 * core + chip
    spot = 4 * y + zl
    owns = spot < PANEL

    load_ao = pltpu.make_async_copy(ao_hbm, ao, load_sem.at[0])
    load_naf = pltpu.make_async_copy(naf_hbm, naf, load_sem.at[1])
    load_vir = pltpu.make_async_copy(vir_hbm, vir, load_sem.at[2])
    load_vir.start()
    load_ao.start()
    load_naf.start()

    barrier = pltpu.get_barrier_semaphore()

    def greet(row, col):
        pl.semaphore_signal(barrier, inc=1, device_id=(row, col), device_id_type=MESH)

    def in_plane(where):
        return 8 * zh + 2 * (where % 4) + where // 16, 4 * zl + (where // 4) % 4

    def in_line(where):
        return 8 * (where // 4) + i, 4 * (where % 4) + y

    for step in (4, 3, 5, 2, 6, 1, 7):
        greet(*in_line((z + step) % LINE))
    for along in FAR_FIRST:
        for across in FAR_FIRST:
            for other in range(2):
                if along or across or other:
                    greet(*in_plane(16 * ((core + other) % 2) + 4 * ((y + across) % 4) + (x + along) % 4))

    def vir_copy(other):
        return pltpu.make_async_remote_copy(
            src_ref=vsend, dst_ref=coeffs.at[core, chip],
            send_sem=vir_send, recv_sem=vir_recv,
            device_id=in_plane(16 * core + other), device_id_type=MESH,
        )

    pass_copy = pltpu.make_async_remote_copy(
        src_ref=coeffs.at[core], dst_ref=coeffs.at[core],
        send_sem=pass_send, recv_sem=pass_recv,
        device_id=(r + 1 - 2 * core, c), device_id_type=MESH,
    )

    def raw_copy(dest, turn):
        first, last = SPANS[turn]
        return pltpu.make_async_remote_copy(
            src_ref=stage.at[dest, first:last], dst_ref=raw.at[place, first:last],
            send_sem=raw_send.at[turn], recv_sem=raw_recv.at[turn],
            device_id=in_plane(dest), device_id_type=MESH,
        )

    def term_copy(other):
        return pltpu.make_async_remote_copy(
            src_ref=part.at[other], dst_ref=terms.at[z],
            send_sem=term_send, recv_sem=term_recv,
            device_id=in_line(other), device_id_type=MESH,
        )

    def row_copy(other):
        return pltpu.make_async_remote_copy(
            src_ref=unit, dst_ref=rowp.at[spot],
            send_sem=row_send, recv_sem=row_recv.at[y],
            device_id=(r, other), device_id_type=MESH,
        )

    goal = r // 4
    holds = x // 2 == zl % 2
    at_home = zl == goal
    goal_y = r % 4

    def hold_copy(half):
        return pltpu.make_async_remote_copy(
            src_ref=unit, dst_ref=held.at[zl],
            send_sem=hold_send, recv_sem=hold_recv,
            device_id=(8 * half + i, 4 * goal + y), device_id_type=MESH,
        )

    col_span = pl.ds(4 * y, 4)

    def col_here(other):
        return jnp.logical_and(other == x, jnp.logical_and(goal_y == y, core == y // 2))

    def col_copy(other):
        return pltpu.make_async_remote_copy(
            src_ref=held, dst_ref=colp.at[col_span],
            send_sem=col_send, recv_sem=col_recv,
            device_id=(8 * zh + 2 * other + y // 2, 4 * zl + goal_y), device_id_type=MESH,
        )

    half_span = pl.ds(8 * core, 8)
    half_copy = pltpu.make_async_remote_copy(
        src_ref=colp.at[half_span], dst_ref=colp.at[half_span],
        send_sem=half_send, recv_sem=half_recv,
        device_id=(r + 1 - 2 * core, c), device_id_type=MESH,
    )

    def pair_copy(half):
        return pltpu.make_async_remote_copy(
            src_ref=proj.at[1 - core, half], dst_ref=pair.at[half],
            send_sem=pair_send.at[half], recv_sem=pair_recv.at[half],
            device_id=(r + 1 - 2 * core, c), device_id_type=MESH,
        )

    def proj_copy(half, other, sent):
        if sent:
            pltpu.make_async_remote_copy(
                src_ref=sums.at[half, other], dst_ref=projs.at[4 * zh + x],
                send_sem=proj_send, recv_sem=proj_recv,
                device_id=(8 * half + 2 * other + core, c), device_id_type=MESH,
            ).start()

    def wait_bytes(ref, sem):
        pltpu.make_async_copy(ref, ref, sem).wait()

    load_vir.wait()
    tail = vir[16:20, :].astype(F32)
    vsend[0:16, :] = vir[0:16, :]
    vsend[16:32, :] = jnp.concatenate([tail, tail, tail, tail], axis=0).astype(BF16)
    coeffs[core, chip, :, :] = vsend[...]
    load_ao.wait()
    turns = []
    for quarter in range(4):
        ahead = (quarter + 4 - z // 2) % 4
        turns.append(jnp.where(ahead == 0, 3, jnp.where(ahead == 1, 1, jnp.where(ahead == 2, 0, 2))))
    for dest in range(PLANE):
        tails = []
        for quarter in range(4):
            panel = 8 * (quarter // 2) + 2 * (dest % 4) + dest // 16
            start = 960 * panel + 256 * ((dest // 4) % 4) + 128 * (quarter % 2)
            if start % 128 == 0:
                tile = ao[:, start : start + 128].astype(F32)
            else:
                after = min(start + 64, 15360 - 128)
                tile = jnp.concatenate([ao[:, start : start + 64], ao[:, after : after + 64]], axis=1).astype(F32)
            stage[dest, pl.ds(pl.multiple_of(16 + 16 * turns[quarter], 16), 16), :] = tile[0:16].astype(BF16)
            tails.append(tile[16:20])
        stage[dest, 0:16, :] = jnp.concatenate(tails, axis=0).astype(BF16)
    raw[place, :, :] = stage[place, :, :]

    pl.semaphore_wait(barrier, PLANE - 1 + LINE - 1)

    @pl.loop(1, 16)
    def _(step):
        vir_copy((chip + 7 * step) % 16).start()

    for turn in range(len(SPANS)):

        for along in FAR_FIRST:
            for across in FAR_FIRST:
                for other in range(2):
                    if along or across or other:
                        raw_copy(16 * ((core + other) % 2) + 4 * ((y + across) % 4) + (x + along) % 4, turn).start()

    wait_bytes(coeffs.at[core, pl.ds(0, 15)], vir_recv)
    pass_copy.start()
    pass_copy.wait_recv()

    coeff = coeffs[:, :, 0:16, :].reshape(512, 128).T
    coeff_tail = coeffs[:, :, 16:32, :].reshape(512, 128).T.astype(F32)
    which = (lax.broadcasted_iota(jnp.int32, (128, 512), 1) // 4) % 4
    for turn in range(4):
        quarter = (z // 2 + SHIFTS[turn]) % 4
        first, last = SPANS[turn]
        wait_bytes(raw.at[pl.ds(0, PLANE - 1), first:last], raw_recv.at[turn])
        ints = raw[:, 16 * turn + 16 : 16 * turn + 32, :].reshape(512, 128)
        ints_tail = raw[:, 0:16, :].reshape(512, 128)
        picked = jnp.where(which == quarter, coeff_tail, 0.0).astype(BF16)
        half = jnp.dot(coeff, ints, preferred_element_type=F32) + jnp.dot(picked, ints_tail, preferred_element_type=F32)
        half = half.T
        for which_half in range(2):
            other = 2 * quarter + which_half
            part[other, :, :] = half[UNIT * which_half : UNIT * (which_half + 1), :]
            if turn < 3:
                term_copy(other).start()
            else:

                @pl.when(other != z)
                def _():
                    term_copy(other).start()

    terms[z, :, :] = part[z, :, :]
    wait_bytes(terms.at[pl.ds(0, LINE - 1)], term_recv)
    total = terms[0, :, :]
    for s in range(1, LINE):
        total = total + terms[s, :, :]
    unit[...] = total.astype(BF16)

    @pl.when(owns)
    def _():
        pltpu.make_async_copy(unit, rowp.at[spot], row_recv.at[y]).start()

        for along in FAR_FIRST:
            for across in FAR_FIRST:
                if along or across:
                    row_copy(4 * ((zl + along) % 4) + (y + across) % 4).start()

    for half in range(2):

        @pl.when(jnp.logical_and(at_home, zh == half))
        def _():
            pltpu.make_async_copy(unit, held.at[zl], hold_recv).start()

        @pl.when(jnp.logical_not(jnp.logical_and(at_home, zh == half)))
        def _():
            hold_copy(half).start()

    @pl.when(holds)
    def _():
        wait_bytes(held, hold_recv)

        @pl.loop(0, 4)
        def _(step):
            other = (x + step) % 4

            @pl.when(col_here(other))
            def _():
                pltpu.make_async_copy(held, colp.at[col_span], col_recv).start()

            @pl.when(jnp.logical_not(col_here(other)))
            def _():
                col_copy(other).start()

    load_naf.wait()
    for group in range(4):
        have = slice(4 * group, min(4 * group + 4, PANEL))
        wait_bytes(rowp.at[have], row_recv.at[group])
    rows = rowp[...].reshape(PANEL * UNIT, 128)
    share = lax.dot_general(rows, naf[...], (((0,), (1,)), ((), ())), preferred_element_type=F32)
    for other in range(16):
        proj[other % 2, other // 8, (other // 2) % 4, :, :] = share[8 * other : 8 * other + 8, :]
    pair_copy(1 - zh).start()
    pair_copy(zh).start()
    for half in (1 - zh, zh):
        pair_copy(half).wait_recv()
        sums[half, :, :, :] = proj[core, half] + pair[half]
        for step in FAR_FIRST:
            proj_copy(half, (x + step) % 4, half is not zh or step != 0)
    projs[4 * zh + x, :, :] = sums[zh, x]

    wait_bytes(colp.at[half_span], col_recv)
    half_copy.start()
    half_copy.wait_recv()
    cols = colp[0:PANEL, :, :].reshape(PANEL * UNIT, 128)
    for band in range(5):
        block = rowp[3 * band : 3 * band + 3, :, :].reshape(3 * UNIT, 128)
        gram_ref[3 * UNIT * band : 3 * UNIT * (band + 1), :] = contract_second(block, cols) * (1.0 / 128)

    wait_bytes(coeffs.at[core, pl.ds(0, 15)], vir_send)
    pass_copy.wait_send()
    for turn in range(len(SPANS)):
        first, last = SPANS[turn]
        wait_bytes(stage.at[pl.ds(0, PLANE - 1), first:last], raw_send.at[turn])
    wait_bytes(part.at[pl.ds(0, LINE - 1)], term_send)

    @pl.when(owns)
    def _():
        wait_bytes(rowp, row_send)

    for count in range(1, 3):

        @pl.when(jnp.where(at_home, 1, 2) == count)
        def _():
            wait_bytes(held.at[0:count], hold_send)

    for count in range(3, 5):

        @pl.when(jnp.logical_and(holds, jnp.where(col_here(x), 3, 4) == count))
        def _():
            wait_bytes(terms.at[0 : 2 * count], col_send)

    half_copy.wait_send()
    for half in range(2):
        pair_copy(half).wait_send()
    wait_bytes(projs.at[pl.ds(0, 7)], proj_recv)
    total = projs[0, :, :]
    for s in range(1, 8):
        total = total + projs[s, :, :]
    naf_ref[...] = total

    wait_bytes(projs.at[pl.ds(0, 7)], proj_send)


BANDS = 8


def spill(gram_ref, naf_ref, gram_hbm, naf_hbm, sems):
    rows = gram_ref.shape[0] // BANDS
    copies = [pltpu.make_async_copy(naf_ref, naf_hbm, sems.at[BANDS])]
    for band in range(BANDS):
        span = pl.ds(rows * band, rows)
        copies.append(pltpu.make_async_copy(gram_ref.at[span], gram_hbm.at[span], sems.at[band]))
    for copy in copies:
        copy.start()
    for copy in copies:
        copy.wait()


def shards(ao_ints, vir_coef, naf_vectors):
    dma = pltpu.SemaphoreType.DMA
    hbm = pl.BlockSpec(memory_space=pltpu.HBM)
    gram, naf_ints = pl.pallas_call(
        kernel,
        out_shape=(
            jax.ShapeDtypeStruct((960, 960), F32),
            jax.ShapeDtypeStruct((8, 448), F32),
        ),
        in_specs=[hbm, hbm, hbm],
        out_specs=(
            pl.BlockSpec(memory_space=pltpu.VMEM),
            pl.BlockSpec(memory_space=pltpu.VMEM),
        ),
        scratch_shapes=[
            pltpu.VMEM((20, 15360), BF16),
            pltpu.VMEM((20, 128), BF16),
            pltpu.VMEM((448, 960), BF16),
            pltpu.VMEM((PLANE, 80, 128), BF16),
            pltpu.VMEM((PLANE, 80, 128), BF16),
            pltpu.VMEM((32, 128), BF16),
            pltpu.VMEM((2, 16, 32, 128), BF16),
            pltpu.VMEM((LINE, UNIT, 128), F32),
            pltpu.VMEM((LINE, UNIT, 128), F32),
            pltpu.VMEM((UNIT, 128), BF16),
            pltpu.VMEM((PANEL, UNIT, 128), BF16),
            pltpu.VMEM((4, UNIT, 128), BF16),
            pltpu.VMEM((16, UNIT, 128), BF16),
            pltpu.VMEM((2, 2, 4, 8, 448), F32),
            pltpu.VMEM((2, 4, 8, 448), F32),
            pltpu.VMEM((2, 4, 8, 448), F32),
            pltpu.VMEM((8, 8, 448), F32),
            dma((3,)), dma, dma, dma, dma, dma((4,)), dma((4,)), dma, dma,
            dma, dma((4,)), dma, dma, dma, dma, dma, dma, dma((2,)), dma((2,)), dma, dma,
        ],
        compiler_params=pltpu.CompilerParams(
            collective_id=0, has_side_effects=True, vmem_limit_bytes=40 * 1024 * 1024
        ),
        name="gram_and_projection",
    )(*(pltpu.with_memory_space_constraint(a, pltpu.HBM) for a in (ao_ints, vir_coef, naf_vectors.T)))
    return pl.pallas_call(
        spill,
        out_shape=(
            jax.ShapeDtypeStruct((960, 960), F32),
            jax.ShapeDtypeStruct((8, 448), F32),
        ),
        in_specs=[pl.BlockSpec(memory_space=pltpu.VMEM)] * 2,
        out_specs=(hbm, hbm),
        scratch_shapes=[dma((BANDS + 1,))],
        compiler_params=pltpu.CompilerParams(vmem_limit_bytes=16 * 1024 * 1024),
        name="spill",
    )(gram, naf_ints)


def solution(mesh):
    in_specs = (P(("row", "col"), None), P(("row", "col"), None), P("row", "col"))
    out_specs = (P("row", "col"), P("row", "col"))
    return jax.shard_map(shards, mesh=mesh, in_specs=in_specs, out_specs=out_specs, check_vma=False)
```

```python
import jax
import jax.numpy as jnp
from jax import lax
from jax.experimental import pallas as pl
from jax.experimental.pallas import tpu as pltpu
from jax.sharding import PartitionSpec as P

MESH = pl.DeviceIdType.MESH
F32 = jnp.float32
BF16 = jnp.bfloat16

LINE = 8
PLANE = 32
UNIT = 64
PANEL = 15
SHIFTS = (2, 1, 3, 0)
SPANS = ((0, 32), (32, 48), (48, 64), (64, 80))
FAR_FIRST = (2, 1, 3, 0)


def contract_first(lhs, rhs):
    return lax.dot_general(lhs, rhs, (((0,), (0,)), ((), ())), preferred_element_type=F32)


def contract_second(lhs, rhs):
    return lax.dot_general(lhs, rhs, (((1,), (1,)), ((), ())), preferred_element_type=F32)


def kernel(
    ao_hbm, vir_hbm, naf_hbm, gram_ref, naf_ref,
    ao, vir, naf, stage, raw, vsend, coeffs, part, terms, unit, rowp, held, colp, proj, pair, sums, projs,
    load_sem, vir_send, vir_recv, pass_send, pass_recv, raw_send, raw_recv, term_send, term_recv,
    row_send, row_recv, hold_send, hold_recv, col_send, col_recv, half_send, half_recv, pair_send, pair_recv, proj_send, proj_recv, meet,
):
    r = lax.axis_index("row")
    c = lax.axis_index("col")
    zh, x, core, zl, y = r // 8, (r // 2) % 4, r % 2, c // 4, c % 4
    i = 2 * x + core
    z = 4 * zh + zl
    chip = 4 * y + x
    place = 16 * core + chip
    spot = 4 * y + zl
    owns = spot < PANEL

    load_ao = pltpu.make_async_copy(ao_hbm, ao, load_sem.at[0])
    load_naf = pltpu.make_async_copy(naf_hbm, naf, load_sem.at[1])
    load_vir = pltpu.make_async_copy(vir_hbm, vir, load_sem.at[2])

    barrier = pltpu.get_barrier_semaphore()

    def greet(row, col):
        pl.semaphore_signal(barrier, inc=1, device_id=(row, col), device_id_type=MESH)

    def in_plane(where):
        return 8 * zh + 2 * (where % 4) + where // 16, 4 * zl + (where // 4) % 4

    def in_line(where):
        return 8 * (where // 4) + i, 4 * (where % 4) + y

    for step in (1, 7):
        greet(*in_line((z + step) % LINE))
    for along in FAR_FIRST:
        for across in FAR_FIRST:
            for other in range(2):
                if along or across or other:
                    greet(*in_plane(16 * ((core + other) % 2) + 4 * ((y + across) % 4) + (x + along) % 4))
    load_vir.start()
    load_ao.start()
    load_naf.start()

    def vir_copy(other):
        return pltpu.make_async_remote_copy(
            src_ref=vsend, dst_ref=coeffs.at[core, chip],
            send_sem=vir_send, recv_sem=vir_recv,
            device_id=in_plane(16 * core + other), device_id_type=MESH,
        )

    pass_copy = pltpu.make_async_remote_copy(
        src_ref=coeffs.at[core], dst_ref=coeffs.at[core],
        send_sem=pass_send, recv_sem=pass_recv,
        device_id=(r + 1 - 2 * core, c), device_id_type=MESH,
    )

    def raw_copy(dest, turn):
        first, last = SPANS[turn]
        return pltpu.make_async_remote_copy(
            src_ref=stage.at[dest, first:last], dst_ref=raw.at[place, first:last],
            send_sem=raw_send.at[turn], recv_sem=raw_recv.at[turn],
            device_id=in_plane(dest), device_id_type=MESH,
        )

    def term_copy(other):
        return pltpu.make_async_remote_copy(
            src_ref=part.at[other], dst_ref=terms.at[z],
            send_sem=term_send, recv_sem=term_recv,
            device_id=in_line(other), device_id_type=MESH,
        )

    def row_copy(other):
        return pltpu.make_async_remote_copy(
            src_ref=unit, dst_ref=rowp.at[spot],
            send_sem=row_send, recv_sem=row_recv.at[y],
            device_id=(r, other), device_id_type=MESH,
        )

    goal = r // 4
    holds = x // 2 == zl % 2
    at_home = zl == goal
    goal_y = r % 4

    def hold_copy(half):
        return pltpu.make_async_remote_copy(
            src_ref=unit, dst_ref=held.at[zl],
            send_sem=hold_send, recv_sem=hold_recv,
            device_id=(8 * half + i, 4 * goal + y), device_id_type=MESH,
        )

    col_span = pl.ds(4 * y, 4)

    def col_here(other):
        return jnp.logical_and(other == x, jnp.logical_and(goal_y == y, core == y // 2))

    def col_copy(other):
        return pltpu.make_async_remote_copy(
            src_ref=held, dst_ref=colp.at[col_span],
            send_sem=col_send, recv_sem=col_recv,
            device_id=(8 * zh + 2 * other + y // 2, 4 * zl + goal_y), device_id_type=MESH,
        )

    half_span = pl.ds(8 * core, 8)
    half_copy = pltpu.make_async_remote_copy(
        src_ref=colp.at[half_span], dst_ref=colp.at[half_span],
        send_sem=half_send, recv_sem=half_recv,
        device_id=(r + 1 - 2 * core, c), device_id_type=MESH,
    )

    def pair_copy(half):
        return pltpu.make_async_remote_copy(
            src_ref=proj.at[1 - core, half], dst_ref=pair.at[half],
            send_sem=pair_send.at[half], recv_sem=pair_recv.at[half],
            device_id=(r + 1 - 2 * core, c), device_id_type=MESH,
        )

    def proj_copy(half, other, sent):
        if sent:
            pltpu.make_async_remote_copy(
                src_ref=sums.at[half, other], dst_ref=projs.at[4 * zh + x],
                send_sem=proj_send, recv_sem=proj_recv,
                device_id=(8 * half + 2 * other + core, c), device_id_type=MESH,
            ).start()

    def wait_bytes(ref, sem):
        pltpu.make_async_copy(ref, ref, sem).wait()

    load_vir.wait()
    tail = vir[16:20, :].astype(F32)
    vsend[0:16, :] = vir[0:16, :]
    vsend[16:32, :] = jnp.concatenate([tail, tail, tail, tail], axis=0).astype(BF16)
    coeffs[core, chip, :, :] = vsend[...]
    load_ao.wait()
    turns = []
    for quarter in range(4):
        ahead = (quarter + 4 - z // 2) % 4
        turns.append(jnp.where(ahead == 0, 3, jnp.where(ahead == 1, 1, jnp.where(ahead == 2, 0, 2))))
    for dest in range(PLANE):
        tails = []
        for quarter in range(4):
            panel = 8 * (quarter // 2) + 2 * (dest % 4) + dest // 16
            start = 960 * panel + 256 * ((dest // 4) % 4) + 128 * (quarter % 2)
            if start % 128 == 0:
                tile = ao[:, start : start + 128].astype(F32)
            else:
                after = min(start + 64, 15360 - 128)
                tile = jnp.concatenate([ao[:, start : start + 64], ao[:, after : after + 64]], axis=1).astype(F32)
            stage[dest, pl.ds(pl.multiple_of(16 + 16 * turns[quarter], 16), 16), :] = tile[0:16].astype(BF16)
            tails.append(tile[16:20])
        stage[dest, 0:16, :] = jnp.concatenate(tails, axis=0).astype(BF16)
    raw[place, :, :] = stage[place, :, :]

    pl.semaphore_wait(barrier, PLANE - 1 + 2)

    def tell(turn, step):
        pl.semaphore_signal(meet.at[turn], inc=1, device_id=in_line((z + step) % LINE), device_id_type=MESH)

    tell(0, 1)
    tell(0, 7)

    @pl.loop(1, 16)
    def _(step):
        vir_copy((chip + 7 * step) % 16).start()

    for turn in range(len(SPANS)):

        for along in FAR_FIRST:
            for across in FAR_FIRST:
                for other in range(2):
                    if along or across or other:
                        raw_copy(16 * ((core + other) % 2) + 4 * ((y + across) % 4) + (x + along) % 4, turn).start()

    pl.semaphore_wait(meet.at[0], 2)
    tell(1, 2)
    tell(1, 6)
    wait_bytes(coeffs.at[core, pl.ds(0, 15)], vir_recv)
    pass_copy.start()
    pl.semaphore_wait(meet.at[1], 2)
    pass_copy.wait_recv()

    coeff = coeffs[:, :, 0:16, :].reshape(512, 128).T
    coeff_tail = coeffs[:, :, 16:32, :].reshape(512, 128).T.astype(F32)
    which = (lax.broadcasted_iota(jnp.int32, (128, 512), 1) // 4) % 4
    for turn in range(4):
        quarter = (z // 2 + SHIFTS[turn]) % 4
        first, last = SPANS[turn]
        wait_bytes(raw.at[pl.ds(0, PLANE - 1), first:last], raw_recv.at[turn])
        ints = raw[:, 16 * turn + 16 : 16 * turn + 32, :].reshape(512, 128)
        ints_tail = raw[:, 0:16, :].reshape(512, 128)
        picked = jnp.where(which == quarter, coeff_tail, 0.0).astype(BF16)
        half = jnp.dot(coeff, ints, preferred_element_type=F32) + jnp.dot(picked, ints_tail, preferred_element_type=F32)
        half = half.T
        for which_half in range(2):
            other = 2 * quarter + which_half
            part[other, :, :] = half[UNIT * which_half : UNIT * (which_half + 1), :]
            if turn < 3:
                term_copy(other).start()
            else:

                @pl.when(other != z)
                def _():
                    term_copy(other).start()

    terms[z, :, :] = part[z, :, :]
    wait_bytes(terms.at[pl.ds(0, LINE - 1)], term_recv)
    total = terms[0, :, :]
    for s in range(1, LINE):
        total = total + terms[s, :, :]
    unit[...] = total.astype(BF16)

    @pl.when(owns)
    def _():
        pltpu.make_async_copy(unit, rowp.at[spot], row_recv.at[y]).start()

        for along in FAR_FIRST:
            for across in FAR_FIRST:
                if along or across:
                    row_copy(4 * ((zl + along) % 4) + (y + across) % 4).start()

    for half in range(2):

        @pl.when(jnp.logical_and(at_home, zh == half))
        def _():
            pltpu.make_async_copy(unit, held.at[zl], hold_recv).start()

        @pl.when(jnp.logical_not(jnp.logical_and(at_home, zh == half)))
        def _():
            hold_copy(half).start()

    load_naf.wait()
    for group in range(4):
        have = slice(4 * group, min(4 * group + 4, PANEL))
        wait_bytes(rowp.at[have], row_recv.at[group])
    rows = rowp[...].reshape(PANEL * UNIT, 128)
    share = lax.dot_general(rows, naf[...], (((0,), (1,)), ((), ())), preferred_element_type=F32)
    for other in range(16):
        proj[other % 2, other // 8, (other // 2) % 4, :, :] = share[8 * other : 8 * other + 8, :]
    pair_copy(1 - zh).start()
    pair_copy(zh).start()
    @pl.when(holds)
    def _():
        wait_bytes(held, hold_recv)

        @pl.loop(0, 4)
        def _(step):
            other = (x + step) % 4

            @pl.when(col_here(other))
            def _():
                pltpu.make_async_copy(held, colp.at[col_span], col_recv).start()

            @pl.when(jnp.logical_not(col_here(other)))
            def _():
                col_copy(other).start()

    for half in (1 - zh, zh):
        pair_copy(half).wait_recv()
        sums[half, :, :, :] = proj[core, half] + pair[half]
        for step in FAR_FIRST:
            proj_copy(half, (x + step) % 4, half is not zh or step != 0)
    projs[4 * zh + x, :, :] = sums[zh, x]

    wait_bytes(colp.at[half_span], col_recv)
    half_copy.start()
    half_copy.wait_recv()
    cols = colp[0:PANEL, :, :].reshape(PANEL * UNIT, 128)
    for band in range(5):
        block = rowp[3 * band : 3 * band + 3, :, :].reshape(3 * UNIT, 128)
        gram_ref[3 * UNIT * band : 3 * UNIT * (band + 1), :] = contract_second(block, cols) * (1.0 / 128)

    wait_bytes(coeffs.at[core, pl.ds(0, 15)], vir_send)
    pass_copy.wait_send()
    for turn in range(len(SPANS)):
        first, last = SPANS[turn]
        wait_bytes(stage.at[pl.ds(0, PLANE - 1), first:last], raw_send.at[turn])
    wait_bytes(part.at[pl.ds(0, LINE - 1)], term_send)

    @pl.when(owns)
    def _():
        wait_bytes(rowp, row_send)

    for count in range(1, 3):

        @pl.when(jnp.where(at_home, 1, 2) == count)
        def _():
            wait_bytes(held.at[0:count], hold_send)

    for count in range(3, 5):

        @pl.when(jnp.logical_and(holds, jnp.where(col_here(x), 3, 4) == count))
        def _():
            wait_bytes(terms.at[0 : 2 * count], col_send)

    half_copy.wait_send()
    for half in range(2):
        pair_copy(half).wait_send()
    wait_bytes(projs.at[pl.ds(0, 7)], proj_recv)
    total = projs[0, :, :]
    for s in range(1, 8):
        total = total + projs[s, :, :]
    naf_ref[...] = total

    wait_bytes(projs.at[pl.ds(0, 7)], proj_send)


BANDS = 8


def spill(gram_ref, naf_ref, gram_hbm, naf_hbm, sems):
    rows = gram_ref.shape[0] // BANDS
    copies = [pltpu.make_async_copy(naf_ref, naf_hbm, sems.at[BANDS])]
    for band in range(BANDS):
        span = pl.ds(rows * band, rows)
        copies.append(pltpu.make_async_copy(gram_ref.at[span], gram_hbm.at[span], sems.at[band]))
    for copy in copies:
        copy.start()
    for copy in copies:
        copy.wait()


def shards(ao_ints, vir_coef, naf_vectors):
    dma = pltpu.SemaphoreType.DMA
    hbm = pl.BlockSpec(memory_space=pltpu.HBM)
    gram, naf_ints = pl.pallas_call(
        kernel,
        out_shape=(
            jax.ShapeDtypeStruct((960, 960), F32),
            jax.ShapeDtypeStruct((8, 448), F32),
        ),
        in_specs=[hbm, hbm, hbm],
        out_specs=(
            pl.BlockSpec(memory_space=pltpu.VMEM),
            pl.BlockSpec(memory_space=pltpu.VMEM),
        ),
        scratch_shapes=[
            pltpu.VMEM((20, 15360), BF16),
            pltpu.VMEM((20, 128), BF16),
            pltpu.VMEM((448, 960), BF16),
            pltpu.VMEM((PLANE, 80, 128), BF16),
            pltpu.VMEM((PLANE, 80, 128), BF16),
            pltpu.VMEM((32, 128), BF16),
            pltpu.VMEM((2, 16, 32, 128), BF16),
            pltpu.VMEM((LINE, UNIT, 128), F32),
            pltpu.VMEM((LINE, UNIT, 128), F32),
            pltpu.VMEM((UNIT, 128), BF16),
            pltpu.VMEM((PANEL, UNIT, 128), BF16),
            pltpu.VMEM((4, UNIT, 128), BF16),
            pltpu.VMEM((16, UNIT, 128), BF16),
            pltpu.VMEM((2, 2, 4, 8, 448), F32),
            pltpu.VMEM((2, 4, 8, 448), F32),
            pltpu.VMEM((2, 4, 8, 448), F32),
            pltpu.VMEM((8, 8, 448), F32),
            dma((3,)), dma, dma, dma, dma, dma((4,)), dma((4,)), dma, dma,
            dma, dma((4,)), dma, dma, dma, dma, dma, dma, dma((2,)), dma((2,)), dma, dma,
            pltpu.SemaphoreType.REGULAR((2,)),
        ],
        compiler_params=pltpu.CompilerParams(
            collective_id=0, has_side_effects=True, vmem_limit_bytes=40 * 1024 * 1024
        ),
        name="gram_and_projection",
    )(*(pltpu.with_memory_space_constraint(a, pltpu.HBM) for a in (ao_ints, vir_coef, naf_vectors.T)))
    return pl.pallas_call(
        spill,
        out_shape=(
            jax.ShapeDtypeStruct((960, 960), F32),
            jax.ShapeDtypeStruct((8, 448), F32),
        ),
        in_specs=[pl.BlockSpec(memory_space=pltpu.VMEM)] * 2,
        out_specs=(hbm, hbm),
        scratch_shapes=[dma((BANDS + 1,))],
        compiler_params=pltpu.CompilerParams(vmem_limit_bytes=16 * 1024 * 1024),
        name="spill",
    )(gram, naf_ints)


def solution(mesh):
    in_specs = (P(("row", "col"), None), P(("row", "col"), None), P("row", "col"))
    out_specs = (P("row", "col"), P("row", "col"))
    return jax.shard_map(shards, mesh=mesh, in_specs=in_specs, out_specs=out_specs, check_vma=False)
```

```python
import jax
import jax.numpy as jnp
from jax import lax
from jax.experimental import pallas as pl
from jax.experimental.pallas import tpu as pltpu
from jax.sharding import PartitionSpec as P

MESH = pl.DeviceIdType.MESH
F32 = jnp.float32
BF16 = jnp.bfloat16

LINE = 8
PLANE = 32
UNIT = 64
PANEL = 15
SHIFTS = (2, 1, 3, 0)
SPANS = ((0, 32), (32, 48), (48, 64), (64, 80))
FAR_FIRST = (2, 1, 3, 0)


def contract_first(lhs, rhs):
    return lax.dot_general(lhs, rhs, (((0,), (0,)), ((), ())), preferred_element_type=F32)


def contract_second(lhs, rhs):
    return lax.dot_general(lhs, rhs, (((1,), (1,)), ((), ())), preferred_element_type=F32)


def kernel(
    ao_hbm, vir_hbm, naf_hbm, rowp, colp, naf_ref,
    ao, vir, naf, stage, raw, vsend, coeffs, part, terms, unit, held, proj, pair, sums, projs,
    load_sem, vir_send, vir_recv, pass_send, pass_recv, raw_send, raw_recv, term_send, term_recv,
    row_send, row_recv, hold_send, hold_recv, col_send, col_recv, half_send, half_recv, pair_send, pair_recv, proj_send, proj_recv, meet,
):
    r = lax.axis_index("row")
    c = lax.axis_index("col")
    zh, x, core, zl, y = r // 8, (r // 2) % 4, r % 2, c // 4, c % 4
    i = 2 * x + core
    z = 4 * zh + zl
    chip = 4 * y + x
    place = 16 * core + chip
    spot = 4 * y + zl
    owns = spot < PANEL

    load_ao = pltpu.make_async_copy(ao_hbm, ao, load_sem.at[0])
    load_naf = pltpu.make_async_copy(naf_hbm, naf, load_sem.at[1])
    load_vir = pltpu.make_async_copy(vir_hbm, vir, load_sem.at[2])

    barrier = pltpu.get_barrier_semaphore()

    def greet(row, col):
        pl.semaphore_signal(barrier, inc=1, device_id=(row, col), device_id_type=MESH)

    def in_plane(where):
        return 8 * zh + 2 * (where % 4) + where // 16, 4 * zl + (where // 4) % 4

    def in_line(where):
        return 8 * (where // 4) + i, 4 * (where % 4) + y

    for step in (1, 7):
        greet(*in_line((z + step) % LINE))
    for along in FAR_FIRST:
        for across in FAR_FIRST:
            for other in range(2):
                if along or across or other:
                    greet(*in_plane(16 * ((core + other) % 2) + 4 * ((y + across) % 4) + (x + along) % 4))
    load_vir.start()
    load_ao.start()
    load_naf.start()

    def vir_copy(other):
        return pltpu.make_async_remote_copy(
            src_ref=vsend, dst_ref=coeffs.at[core, chip],
            send_sem=vir_send, recv_sem=vir_recv,
            device_id=in_plane(16 * core + other), device_id_type=MESH,
        )

    pass_copy = pltpu.make_async_remote_copy(
        src_ref=coeffs.at[core], dst_ref=coeffs.at[core],
        send_sem=pass_send, recv_sem=pass_recv,
        device_id=(r + 1 - 2 * core, c), device_id_type=MESH,
    )

    def raw_copy(dest, turn):
        first, last = SPANS[turn]
        return pltpu.make_async_remote_copy(
            src_ref=stage.at[dest, first:last], dst_ref=raw.at[place, first:last],
            send_sem=raw_send.at[turn], recv_sem=raw_recv.at[turn],
            device_id=in_plane(dest), device_id_type=MESH,
        )

    def term_copy(other):
        return pltpu.make_async_remote_copy(
            src_ref=part.at[other], dst_ref=terms.at[z],
            send_sem=term_send, recv_sem=term_recv,
            device_id=in_line(other), device_id_type=MESH,
        )

    def row_copy(other):
        return pltpu.make_async_remote_copy(
            src_ref=unit, dst_ref=rowp.at[spot],
            send_sem=row_send, recv_sem=row_recv.at[y],
            device_id=(r, other), device_id_type=MESH,
        )

    goal = r // 4
    holds = x // 2 == zl % 2
    at_home = zl == goal
    goal_y = r % 4

    def hold_copy(half):
        return pltpu.make_async_remote_copy(
            src_ref=unit, dst_ref=held.at[zl],
            send_sem=hold_send, recv_sem=hold_recv,
            device_id=(8 * half + i, 4 * goal + y), device_id_type=MESH,
        )

    col_span = pl.ds(4 * y, 4)

    def col_here(other):
        return jnp.logical_and(other == x, jnp.logical_and(goal_y == y, core == y // 2))

    def col_copy(other):
        return pltpu.make_async_remote_copy(
            src_ref=held, dst_ref=colp.at[col_span],
            send_sem=col_send, recv_sem=col_recv,
            device_id=(8 * zh + 2 * other + y // 2, 4 * zl + goal_y), device_id_type=MESH,
        )

    half_span = pl.ds(8 * core, 8)
    half_copy = pltpu.make_async_remote_copy(
        src_ref=colp.at[half_span], dst_ref=colp.at[half_span],
        send_sem=half_send, recv_sem=half_recv,
        device_id=(r + 1 - 2 * core, c), device_id_type=MESH,
    )

    def pair_copy(half):
        return pltpu.make_async_remote_copy(
            src_ref=proj.at[1 - core, half], dst_ref=pair.at[half],
            send_sem=pair_send.at[half], recv_sem=pair_recv.at[half],
            device_id=(r + 1 - 2 * core, c), device_id_type=MESH,
        )

    def proj_copy(half, other, sent):
        if sent:
            pltpu.make_async_remote_copy(
                src_ref=sums.at[half, other], dst_ref=projs.at[4 * zh + x],
                send_sem=proj_send, recv_sem=proj_recv,
                device_id=(8 * half + 2 * other + core, c), device_id_type=MESH,
            ).start()

    def wait_bytes(ref, sem):
        pltpu.make_async_copy(ref, ref, sem).wait()

    load_vir.wait()
    tail = vir[16:20, :].astype(F32)
    vsend[0:16, :] = vir[0:16, :]
    vsend[16:24, :] = jnp.concatenate([tail, tail], axis=0).astype(BF16)
    coeffs[core, chip, :, :] = vsend[...]
    load_ao.wait()
    turns = []
    for quarter in range(4):
        ahead = (quarter + 4 - z // 2) % 4
        turns.append(jnp.where(ahead == 0, 3, jnp.where(ahead == 1, 1, jnp.where(ahead == 2, 0, 2))))
    for dest in range(PLANE):
        tails = []
        for quarter in range(4):
            panel = 8 * (quarter // 2) + 2 * (dest % 4) + dest // 16
            start = 960 * panel + 256 * ((dest // 4) % 4) + 128 * (quarter % 2)
            if start % 128 == 0:
                tile = ao[:, start : start + 128].astype(F32)
            else:
                after = min(start + 64, 15360 - 128)
                tile = jnp.concatenate([ao[:, start : start + 64], ao[:, after : after + 64]], axis=1).astype(F32)
            stage[dest, pl.ds(pl.multiple_of(16 + 16 * turns[quarter], 16), 16), :] = tile[0:16].astype(BF16)
            tails.append(tile[16:20])
        stage[dest, 0:16, :] = jnp.concatenate(tails, axis=0).astype(BF16)
    raw[place, :, :] = stage[place, :, :]

    pl.semaphore_wait(barrier, PLANE - 1 + 2)

    def tell(turn, step):
        pl.semaphore_signal(meet.at[turn], inc=1, device_id=in_line((z + step) % LINE), device_id_type=MESH)

    tell(0, 1)
    tell(0, 7)

    for along in FAR_FIRST:
        for across in FAR_FIRST:
            if along or across:
                vir_copy(4 * ((y + across) % 4) + (x + along) % 4).start()

    for turn in range(len(SPANS)):

        for along in FAR_FIRST:
            for across in FAR_FIRST:
                for other in range(2):
                    if along or across or other:
                        raw_copy(16 * ((core + other) % 2) + 4 * ((y + across) % 4) + (x + along) % 4, turn).start()

    pl.semaphore_wait(meet.at[0], 2)
    tell(1, 2)
    tell(1, 6)
    wait_bytes(coeffs.at[core, pl.ds(0, 15)], vir_recv)
    pass_copy.start()
    pl.semaphore_wait(meet.at[1], 2)
    pass_copy.wait_recv()

    coeff = coeffs[:, :, 0:16, :].reshape(512, 128).T
    coeff_tail = coeffs[:, :, 16:24, :].astype(F32)
    coeff_tail = jnp.concatenate([coeff_tail, coeff_tail], axis=2).reshape(512, 128).T
    which = (lax.broadcasted_iota(jnp.int32, (128, 512), 1) // 4) % 4
    for turn in range(4):
        quarter = (z // 2 + SHIFTS[turn]) % 4
        first, last = SPANS[turn]
        wait_bytes(raw.at[pl.ds(0, PLANE - 1), first:last], raw_recv.at[turn])
        ints = raw[:, 16 * turn + 16 : 16 * turn + 32, :].reshape(512, 128)
        ints_tail = raw[:, 0:16, :].reshape(512, 128)
        picked = jnp.where(which == quarter, coeff_tail, 0.0).astype(BF16)
        half = jnp.dot(coeff, ints, preferred_element_type=F32) + jnp.dot(picked, ints_tail, preferred_element_type=F32)
        half = half.T
        for which_half in range(2):
            other = 2 * quarter + which_half
            part[other, :, :] = half[UNIT * which_half : UNIT * (which_half + 1), :]
            if turn < 3:
                term_copy(other).start()
            else:

                @pl.when(other != z)
                def _():
                    term_copy(other).start()

    terms[z, :, :] = part[z, :, :]
    wait_bytes(terms.at[pl.ds(0, LINE - 1)], term_recv)
    total = terms[0, :, :]
    for s in range(1, LINE):
        total = total + terms[s, :, :]
    unit[...] = total.astype(BF16)

    @pl.when(owns)
    def _():
        pltpu.make_async_copy(unit, rowp.at[spot], row_recv.at[y]).start()

        for along in FAR_FIRST:
            for across in FAR_FIRST:
                if along or across:
                    row_copy(4 * ((zl + along) % 4) + (y + across) % 4).start()

    for half in range(2):

        @pl.when(jnp.logical_and(at_home, zh == half))
        def _():
            pltpu.make_async_copy(unit, held.at[zl], hold_recv).start()

        @pl.when(jnp.logical_not(jnp.logical_and(at_home, zh == half)))
        def _():
            hold_copy(half).start()

    load_naf.wait()
    for group in range(4):
        have = slice(4 * group, min(4 * group + 4, PANEL))
        wait_bytes(rowp.at[have], row_recv.at[group])
    rows = rowp[...].reshape(PANEL * UNIT, 128)
    share = lax.dot_general(rows, naf[...], (((0,), (1,)), ((), ())), preferred_element_type=F32)
    for other in range(16):
        proj[other % 2, other // 8, (other // 2) % 4, :, :] = share[8 * other : 8 * other + 8, :]
    pair_copy(1 - zh).start()
    pair_copy(zh).start()
    @pl.when(holds)
    def _():
        wait_bytes(held, hold_recv)

        @pl.loop(0, 4)
        def _(step):
            other = (x + 2 + 3 * step) % 4

            @pl.when(col_here(other))
            def _():
                pltpu.make_async_copy(held, colp.at[col_span], col_recv).start()

            @pl.when(jnp.logical_not(col_here(other)))
            def _():
                col_copy(other).start()

    for half in (1 - zh, zh):
        pair_copy(half).wait_recv()
        sums[half, :, :, :] = proj[core, half] + pair[half]
        for step in FAR_FIRST:
            proj_copy(half, (x + step) % 4, half is not zh or step != 0)
    projs[4 * zh + x, :, :] = sums[zh, x]

    wait_bytes(colp.at[half_span], col_recv)
    half_copy.start()
    half_copy.wait_recv()
    wait_bytes(coeffs.at[core, pl.ds(0, 15)], vir_send)
    pass_copy.wait_send()
    for turn in range(len(SPANS)):
        first, last = SPANS[turn]
        wait_bytes(stage.at[pl.ds(0, PLANE - 1), first:last], raw_send.at[turn])
    wait_bytes(part.at[pl.ds(0, LINE - 1)], term_send)

    @pl.when(owns)
    def _():
        wait_bytes(rowp, row_send)

    for count in range(1, 3):

        @pl.when(jnp.where(at_home, 1, 2) == count)
        def _():
            wait_bytes(held.at[0:count], hold_send)

    for count in range(3, 5):

        @pl.when(jnp.logical_and(holds, jnp.where(col_here(x), 3, 4) == count))
        def _():
            wait_bytes(terms.at[0 : 2 * count], col_send)

    half_copy.wait_send()
    for half in range(2):
        pair_copy(half).wait_send()
    wait_bytes(projs.at[pl.ds(0, 7)], proj_recv)
    total = projs[0, :, :]
    for s in range(1, 8):
        total = total + projs[s, :, :]
    naf_ref[...] = total

    wait_bytes(projs.at[pl.ds(0, 7)], proj_send)


BANDS = 5


def finish(rowp, colp, naf_ref, gram_hbm, naf_hbm, gram, sems):
    pltpu.make_async_copy(naf_ref, naf_hbm, sems.at[BANDS]).start()
    cols = colp[0:PANEL, :, :].reshape(PANEL * UNIT, 128)
    rows = PANEL * UNIT // BANDS
    copies = []
    for band in range(BANDS):
        block = rowp[3 * band : 3 * band + 3, :, :].reshape(rows, 128)
        gram[rows * band : rows * (band + 1), :] = contract_second(block, cols) * (1.0 / 128)
        span = pl.ds(rows * band, rows)
        copies.append(pltpu.make_async_copy(gram.at[span], gram_hbm.at[span], sems.at[band]))
        copies[-1].start()
    for copy in copies:
        copy.wait()
    pltpu.make_async_copy(naf_ref, naf_hbm, sems.at[BANDS]).wait()


def shards(ao_ints, vir_coef, naf_vectors):
    dma = pltpu.SemaphoreType.DMA
    hbm = pl.BlockSpec(memory_space=pltpu.HBM)
    rowp, colp, naf_ints = pl.pallas_call(
        kernel,
        out_shape=(
            jax.ShapeDtypeStruct((PANEL, UNIT, 128), BF16),
            jax.ShapeDtypeStruct((16, UNIT, 128), BF16),
            jax.ShapeDtypeStruct((8, 448), F32),
        ),
        in_specs=[hbm, hbm, hbm],
        out_specs=[pl.BlockSpec(memory_space=pltpu.VMEM)] * 3,
        scratch_shapes=[
            pltpu.VMEM((20, 15360), BF16),
            pltpu.VMEM((20, 128), BF16),
            pltpu.VMEM((448, 960), BF16),
            pltpu.VMEM((PLANE, 80, 128), BF16),
            pltpu.VMEM((PLANE, 80, 128), BF16),
            pltpu.VMEM((24, 128), BF16),
            pltpu.VMEM((2, 16, 24, 128), BF16),
            pltpu.VMEM((LINE, UNIT, 128), F32),
            pltpu.VMEM((LINE, UNIT, 128), F32),
            pltpu.VMEM((UNIT, 128), BF16),
            pltpu.VMEM((4, UNIT, 128), BF16),
            pltpu.VMEM((2, 2, 4, 8, 448), F32),
            pltpu.VMEM((2, 4, 8, 448), F32),
            pltpu.VMEM((2, 4, 8, 448), F32),
            pltpu.VMEM((8, 8, 448), F32),
            dma((3,)), dma, dma, dma, dma, dma((4,)), dma((4,)), dma, dma,
            dma, dma((4,)), dma, dma, dma, dma, dma, dma, dma((2,)), dma((2,)), dma, dma,
            pltpu.SemaphoreType.REGULAR((2,)),
        ],
        compiler_params=pltpu.CompilerParams(
            collective_id=0, has_side_effects=True, vmem_limit_bytes=40 * 1024 * 1024
        ),
        name="panels_and_projection",
    )(*(pltpu.with_memory_space_constraint(a, pltpu.HBM) for a in (ao_ints, vir_coef, naf_vectors.T)))
    return pl.pallas_call(
        finish,
        out_shape=(
            jax.ShapeDtypeStruct((960, 960), F32),
            jax.ShapeDtypeStruct((8, 448), F32),
        ),
        in_specs=[pl.BlockSpec(memory_space=pltpu.VMEM)] * 3,
        out_specs=(hbm, hbm),
        scratch_shapes=[pltpu.VMEM((960, 960), F32), dma((BANDS + 1,))],
        compiler_params=pltpu.CompilerParams(vmem_limit_bytes=16 * 1024 * 1024),
        name="gram",
    )(rowp, colp, naf_ints)


def solution(mesh):
    in_specs = (P(("row", "col"), None), P(("row", "col"), None), P("row", "col"))
    out_specs = (P("row", "col"), P("row", "col"))
    return jax.shard_map(shards, mesh=mesh, in_specs=in_specs, out_specs=out_specs, check_vma=False)
```

```python
import jax
import jax.numpy as jnp
from jax import lax
from jax.experimental import pallas as pl
from jax.experimental.pallas import tpu as pltpu
from jax.sharding import PartitionSpec as P

MESH = pl.DeviceIdType.MESH
F32 = jnp.float32
BF16 = jnp.bfloat16

LINE = 8
PLANE = 32
UNIT = 64
PANEL = 15
SHIFTS = (2, 1, 3, 0)
SPANS = ((0, 32), (32, 48), (48, 64), (64, 80))
FAR_FIRST = (2, 1, 3, 0)


def contract_first(lhs, rhs):
    return lax.dot_general(lhs, rhs, (((0,), (0,)), ((), ())), preferred_element_type=F32)


def contract_second(lhs, rhs):
    return lax.dot_general(lhs, rhs, (((1,), (1,)), ((), ())), preferred_element_type=F32)


def kernel(
    ao_hbm, vir_hbm, naf_hbm, rowp, colp, naf_ref,
    ao, vir, naf, stage, raw, vsend, coeffs, part, terms, unit, held, proj, pair, sums, projs,
    load_sem, vir_send, vir_recv, pass_send, pass_recv, raw_send, raw_recv, term_send, term_recv,
    row_send, row_recv, hold_send, hold_recv, col_send, col_recv, half_send, half_recv, pair_send, pair_recv, proj_send, proj_recv, meet,
):
    r = lax.axis_index("row")
    c = lax.axis_index("col")
    zh, x, core, zl, y = r // 8, (r // 2) % 4, r % 2, c // 4, c % 4
    i = 2 * x + core
    z = 4 * zh + zl
    chip = 4 * y + x
    place = 16 * core + chip
    spot = 4 * y + zl
    owns = spot < PANEL

    load_ao = pltpu.make_async_copy(ao_hbm, ao, load_sem.at[0])
    load_naf = pltpu.make_async_copy(naf_hbm, naf, load_sem.at[1])
    load_vir = pltpu.make_async_copy(vir_hbm, vir, load_sem.at[2])

    barrier = pltpu.get_barrier_semaphore()

    def greet(row, col):
        pl.semaphore_signal(barrier, inc=1, device_id=(row, col), device_id_type=MESH)

    def in_plane(where):
        return 8 * zh + 2 * (where % 4) + where // 16, 4 * zl + (where // 4) % 4

    def in_line(where):
        return 8 * (where // 4) + i, 4 * (where % 4) + y

    for step in (1, 7):
        greet(*in_line((z + step) % LINE))
    for along in FAR_FIRST:
        for across in FAR_FIRST:
            for other in range(2):
                if along or across or other:
                    greet(*in_plane(16 * ((core + other) % 2) + 4 * ((y + across) % 4) + (x + along) % 4))
    load_vir.start()
    load_ao.start()
    load_naf.start()

    def vir_copy(other):
        return pltpu.make_async_remote_copy(
            src_ref=vsend, dst_ref=coeffs.at[core, chip],
            send_sem=vir_send, recv_sem=vir_recv,
            device_id=in_plane(16 * core + other), device_id_type=MESH,
        )

    pass_copy = pltpu.make_async_remote_copy(
        src_ref=coeffs.at[core], dst_ref=coeffs.at[core],
        send_sem=pass_send, recv_sem=pass_recv,
        device_id=(r + 1 - 2 * core, c), device_id_type=MESH,
    )

    def raw_copy(dest, turn):
        first, last = SPANS[turn]
        return pltpu.make_async_remote_copy(
            src_ref=stage.at[dest, first:last], dst_ref=raw.at[place, first:last],
            send_sem=raw_send.at[turn], recv_sem=raw_recv.at[turn],
            device_id=in_plane(dest), device_id_type=MESH,
        )

    def term_copy(other):
        return pltpu.make_async_remote_copy(
            src_ref=part.at[other], dst_ref=terms.at[z],
            send_sem=term_send, recv_sem=term_recv,
            device_id=in_line(other), device_id_type=MESH,
        )

    def row_copy(other):
        return pltpu.make_async_remote_copy(
            src_ref=unit, dst_ref=rowp.at[spot],
            send_sem=row_send, recv_sem=row_recv.at[y],
            device_id=(r, other), device_id_type=MESH,
        )

    goal = r // 4
    holds = x // 2 == zl % 2
    at_home = zl == goal
    goal_y = r % 4

    def hold_copy(half):
        return pltpu.make_async_remote_copy(
            src_ref=unit, dst_ref=held.at[zl],
            send_sem=hold_send, recv_sem=hold_recv,
            device_id=(8 * half + i, 4 * goal + y), device_id_type=MESH,
        )

    col_span = pl.ds(4 * y, 4)

    def col_here(other):
        return jnp.logical_and(other == x, jnp.logical_and(goal_y == y, core == y // 2))

    def col_copy(other):
        return pltpu.make_async_remote_copy(
            src_ref=held, dst_ref=colp.at[col_span],
            send_sem=col_send, recv_sem=col_recv,
            device_id=(8 * zh + 2 * other + y // 2, 4 * zl + goal_y), device_id_type=MESH,
        )

    half_span = pl.ds(8 * core, 8)
    half_copy = pltpu.make_async_remote_copy(
        src_ref=colp.at[half_span], dst_ref=colp.at[half_span],
        send_sem=half_send, recv_sem=half_recv,
        device_id=(r + 1 - 2 * core, c), device_id_type=MESH,
    )

    def pair_copy(half):
        return pltpu.make_async_remote_copy(
            src_ref=proj.at[1 - core, half], dst_ref=pair.at[half],
            send_sem=pair_send.at[half], recv_sem=pair_recv.at[half],
            device_id=(r + 1 - 2 * core, c), device_id_type=MESH,
        )

    def proj_copy(half, other, sent):
        if sent:
            pltpu.make_async_remote_copy(
                src_ref=sums.at[half, other], dst_ref=projs.at[4 * zh + x],
                send_sem=proj_send, recv_sem=proj_recv,
                device_id=(8 * half + 2 * other + core, c), device_id_type=MESH,
            ).start()

    def wait_bytes(ref, sem):
        pltpu.make_async_copy(ref, ref, sem).wait()

    load_vir.wait()
    tail = vir[16:20, :].astype(F32)
    vsend[0:16, :] = vir[0:16, :]
    vsend[16:24, :] = jnp.concatenate([tail, tail], axis=0).astype(BF16)
    coeffs[core, chip, :, :] = vsend[...]
    load_ao.wait()
    turns = []
    for quarter in range(4):
        ahead = (quarter + 4 - z // 2) % 4
        turns.append(jnp.where(ahead == 0, 3, jnp.where(ahead == 1, 1, jnp.where(ahead == 2, 0, 2))))
    for dest in range(PLANE):
        tails = []
        for quarter in range(4):
            panel = 8 * (quarter // 2) + 2 * (dest % 4) + dest // 16
            start = 960 * panel + 256 * ((dest // 4) % 4) + 128 * (quarter % 2)
            if start % 128 == 0:
                tile = ao[:, start : start + 128].astype(F32)
            else:
                after = min(start + 64, 15360 - 128)
                tile = jnp.concatenate([ao[:, start : start + 64], ao[:, after : after + 64]], axis=1).astype(F32)
            stage[dest, pl.ds(pl.multiple_of(16 + 16 * turns[quarter], 16), 16), :] = tile[0:16].astype(BF16)
            tails.append(tile[16:20])
        stage[dest, 0:16, :] = jnp.concatenate(tails, axis=0).astype(BF16)
    raw[place, :, :] = stage[place, :, :]

    pl.semaphore_wait(barrier, PLANE - 1 + 2)

    def tell(turn, step):
        pl.semaphore_signal(meet.at[turn], inc=1, device_id=in_line((z + step) % LINE), device_id_type=MESH)

    tell(0, 1)
    tell(0, 7)

    for along in FAR_FIRST:
        for across in FAR_FIRST:
            if along or across:
                vir_copy(4 * ((y + across) % 4) + (x + along) % 4).start()

    for turn in range(len(SPANS)):

        for along in FAR_FIRST:
            for across in FAR_FIRST:
                for other in range(2):
                    if along or across or other:
                        raw_copy(16 * ((core + other) % 2) + 4 * ((y + across) % 4) + (x + along) % 4, turn).start()

    pl.semaphore_wait(meet.at[0], 2)
    tell(1, 2)
    tell(1, 6)
    wait_bytes(coeffs.at[core, pl.ds(0, 15)], vir_recv)
    pass_copy.start()
    pass_copy.wait_recv()

    coeff = coeffs[:, :, 0:16, :].reshape(512, 128).T
    coeff_tail = coeffs[:, :, 16:24, :].astype(F32)
    coeff_tail = jnp.concatenate([coeff_tail, coeff_tail], axis=2).reshape(512, 128).T
    which = (lax.broadcasted_iota(jnp.int32, (128, 512), 1) // 4) % 4
    for turn in range(4):
        quarter = (z // 2 + SHIFTS[turn]) % 4
        first, last = SPANS[turn]
        wait_bytes(raw.at[pl.ds(0, PLANE - 1), first:last], raw_recv.at[turn])
        ints = raw[:, 16 * turn + 16 : 16 * turn + 32, :].reshape(512, 128)
        ints_tail = raw[:, 0:16, :].reshape(512, 128)
        picked = jnp.where(which == quarter, coeff_tail, 0.0).astype(BF16)
        half = jnp.dot(coeff, ints, preferred_element_type=F32) + jnp.dot(picked, ints_tail, preferred_element_type=F32)
        half = half.T
        if turn == 0:
            pl.semaphore_wait(meet.at[1], 2)
        for which_half in range(2):
            other = 2 * quarter + which_half
            part[other, :, :] = half[UNIT * which_half : UNIT * (which_half + 1), :]
            if turn < 3:
                term_copy(other).start()
            else:

                @pl.when(other != z)
                def _():
                    term_copy(other).start()

    terms[z, :, :] = part[z, :, :]
    wait_bytes(terms.at[pl.ds(0, LINE - 1)], term_recv)
    total = terms[0, :, :]
    for s in range(1, LINE):
        total = total + terms[s, :, :]
    unit[...] = total.astype(BF16)

    @pl.when(owns)
    def _():
        pltpu.make_async_copy(unit, rowp.at[spot], row_recv.at[y]).start()

        for along in FAR_FIRST:
            for across in FAR_FIRST:
                if along or across:
                    row_copy(4 * ((zl + along) % 4) + (y + across) % 4).start()

    for half in range(2):

        @pl.when(jnp.logical_and(at_home, zh == half))
        def _():
            pltpu.make_async_copy(unit, held.at[zl], hold_recv).start()

        @pl.when(jnp.logical_not(jnp.logical_and(at_home, zh == half)))
        def _():
            hold_copy(half).start()

    load_naf.wait()
    for group in range(4):
        have = slice(4 * group, min(4 * group + 4, PANEL))
        wait_bytes(rowp.at[have], row_recv.at[group])
    rows = rowp[...].reshape(PANEL * UNIT, 128)
    share = lax.dot_general(rows, naf[...], (((0,), (1,)), ((), ())), preferred_element_type=F32)
    for other in range(16):
        proj[other % 2, other // 8, (other // 2) % 4, :, :] = share[8 * other : 8 * other + 8, :]
    pair_copy(1 - zh).start()
    pair_copy(zh).start()
    @pl.when(holds)
    def _():
        wait_bytes(held, hold_recv)

        @pl.loop(0, 4)
        def _(step):
            other = (x + 2 + 3 * step) % 4

            @pl.when(col_here(other))
            def _():
                pltpu.make_async_copy(held, colp.at[col_span], col_recv).start()

            @pl.when(jnp.logical_not(col_here(other)))
            def _():
                col_copy(other).start()

    for half in (1 - zh, zh):
        pair_copy(half).wait_recv()
        sums[half, :, :, :] = proj[core, half] + pair[half]
        for step in FAR_FIRST:
            proj_copy(half, (x + step) % 4, half is not zh or step != 0)
    projs[4 * zh + x, :, :] = sums[zh, x]

    wait_bytes(colp.at[half_span], col_recv)
    half_copy.start()
    half_copy.wait_recv()
    wait_bytes(coeffs.at[core, pl.ds(0, 15)], vir_send)
    pass_copy.wait_send()
    for turn in range(len(SPANS)):
        first, last = SPANS[turn]
        wait_bytes(stage.at[pl.ds(0, PLANE - 1), first:last], raw_send.at[turn])
    wait_bytes(part.at[pl.ds(0, LINE - 1)], term_send)

    @pl.when(owns)
    def _():
        wait_bytes(rowp, row_send)

    for count in range(1, 3):

        @pl.when(jnp.where(at_home, 1, 2) == count)
        def _():
            wait_bytes(held.at[0:count], hold_send)

    for count in range(3, 5):

        @pl.when(jnp.logical_and(holds, jnp.where(col_here(x), 3, 4) == count))
        def _():
            wait_bytes(terms.at[0 : 2 * count], col_send)

    half_copy.wait_send()
    for half in range(2):
        pair_copy(half).wait_send()
    wait_bytes(projs.at[pl.ds(0, 7)], proj_recv)
    total = projs[0, :, :]
    for s in range(1, 8):
        total = total + projs[s, :, :]
    naf_ref[...] = total

    wait_bytes(projs.at[pl.ds(0, 7)], proj_send)


BANDS = 5


def finish(rowp, colp, naf_ref, gram_hbm, naf_hbm, gram, sems):
    pltpu.make_async_copy(naf_ref, naf_hbm, sems.at[BANDS]).start()
    cols = colp[0:PANEL, :, :].reshape(PANEL * UNIT, 128)
    rows = PANEL * UNIT // BANDS
    copies = []
    for band in range(BANDS):
        block = rowp[3 * band : 3 * band + 3, :, :].reshape(rows, 128)
        gram[rows * band : rows * (band + 1), :] = contract_second(block, cols) * (1.0 / 128)
        span = pl.ds(rows * band, rows)
        copies.append(pltpu.make_async_copy(gram.at[span], gram_hbm.at[span], sems.at[band]))
        copies[-1].start()
    for copy in copies:
        copy.wait()
    pltpu.make_async_copy(naf_ref, naf_hbm, sems.at[BANDS]).wait()


def shards(ao_ints, vir_coef, naf_vectors):
    dma = pltpu.SemaphoreType.DMA
    hbm = pl.BlockSpec(memory_space=pltpu.HBM)
    rowp, colp, naf_ints = pl.pallas_call(
        kernel,
        out_shape=(
            jax.ShapeDtypeStruct((PANEL, UNIT, 128), BF16),
            jax.ShapeDtypeStruct((16, UNIT, 128), BF16),
            jax.ShapeDtypeStruct((8, 448), F32),
        ),
        in_specs=[hbm, hbm, hbm],
        out_specs=[pl.BlockSpec(memory_space=pltpu.VMEM)] * 3,
        scratch_shapes=[
            pltpu.VMEM((20, 15360), BF16),
            pltpu.VMEM((20, 128), BF16),
            pltpu.VMEM((448, 960), BF16),
            pltpu.VMEM((PLANE, 80, 128), BF16),
            pltpu.VMEM((PLANE, 80, 128), BF16),
            pltpu.VMEM((24, 128), BF16),
            pltpu.VMEM((2, 16, 24, 128), BF16),
            pltpu.VMEM((LINE, UNIT, 128), F32),
            pltpu.VMEM((LINE, UNIT, 128), F32),
            pltpu.VMEM((UNIT, 128), BF16),
            pltpu.VMEM((4, UNIT, 128), BF16),
            pltpu.VMEM((2, 2, 4, 8, 448), F32),
            pltpu.VMEM((2, 4, 8, 448), F32),
            pltpu.VMEM((2, 4, 8, 448), F32),
            pltpu.VMEM((8, 8, 448), F32),
            dma((3,)), dma, dma, dma, dma, dma((4,)), dma((4,)), dma, dma,
            dma, dma((4,)), dma, dma, dma, dma, dma, dma, dma((2,)), dma((2,)), dma, dma,
            pltpu.SemaphoreType.REGULAR((2,)),
        ],
        compiler_params=pltpu.CompilerParams(
            collective_id=0, has_side_effects=True, vmem_limit_bytes=40 * 1024 * 1024
        ),
        name="panels_and_projection",
    )(*(pltpu.with_memory_space_constraint(a, pltpu.HBM) for a in (ao_ints, vir_coef, naf_vectors.T)))
    return pl.pallas_call(
        finish,
        out_shape=(
            jax.ShapeDtypeStruct((960, 960), F32),
            jax.ShapeDtypeStruct((8, 448), F32),
        ),
        in_specs=[pl.BlockSpec(memory_space=pltpu.VMEM)] * 3,
        out_specs=(hbm, hbm),
        scratch_shapes=[pltpu.VMEM((960, 960), F32), dma((BANDS + 1,))],
        compiler_params=pltpu.CompilerParams(vmem_limit_bytes=16 * 1024 * 1024),
        name="gram",
    )(rowp, colp, naf_ints)


def solution(mesh):
    in_specs = (P(("row", "col"), None), P(("row", "col"), None), P("row", "col"))
    out_specs = (P("row", "col"), P("row", "col"))
    return jax.shard_map(shards, mesh=mesh, in_specs=in_specs, out_specs=out_specs, check_vma=False)
```

```python
import jax
import jax.numpy as jnp
from jax import lax
from jax.experimental import pallas as pl
from jax.experimental.pallas import tpu as pltpu
from jax.sharding import PartitionSpec as P

MESH = pl.DeviceIdType.MESH
F32 = jnp.float32
BF16 = jnp.bfloat16

LINE = 8
PLANE = 32
UNIT = 64
PANEL = 15
SHIFTS = (2, 1, 3, 0)
SPANS = ((0, 32), (32, 48), (48, 64), (64, 80))
FAR_FIRST = (2, 1, 3, 0)


def contract_first(lhs, rhs):
    return lax.dot_general(lhs, rhs, (((0,), (0,)), ((), ())), preferred_element_type=F32)


def contract_second(lhs, rhs):
    return lax.dot_general(lhs, rhs, (((1,), (1,)), ((), ())), preferred_element_type=F32)


def kernel(
    ao_hbm, vir_hbm, naf_hbm, rowp, colp, naf_ref,
    ao, vir, naf, stage, raw, vsend, coeffs, part, terms, unit, held, proj, pair, sums, projs,
    load_sem, vir_send, vir_recv, pass_send, pass_recv, raw_send, raw_recv, term_send, term_recv,
    row_send, row_recv, hold_send, hold_recv, col_send, col_recv, half_send, half_recv, pair_send, pair_recv, proj_send, proj_recv, meet,
):
    r = lax.axis_index("row")
    c = lax.axis_index("col")
    zh, x, core, zl, y = r // 8, (r // 2) % 4, r % 2, c // 4, c % 4
    i = 2 * x + core
    z = 4 * zh + zl
    chip = 4 * y + x
    place = 16 * core + chip
    spot = 4 * y + zl
    owns = spot < PANEL

    load_ao = pltpu.make_async_copy(ao_hbm, ao, load_sem.at[0])
    load_naf = pltpu.make_async_copy(naf_hbm, naf, load_sem.at[1])
    load_vir = pltpu.make_async_copy(vir_hbm, vir, load_sem.at[2])

    barrier = pltpu.get_barrier_semaphore()

    def greet(row, col):
        pl.semaphore_signal(barrier, inc=1, device_id=(row, col), device_id_type=MESH)

    def in_plane(where):
        return 8 * zh + 2 * (where % 4) + where // 16, 4 * zl + (where // 4) % 4

    def in_line(where):
        return 8 * (where // 4) + i, 4 * (where % 4) + y

    for step in (1, 7):
        greet(*in_line((z + step) % LINE))
    for along in FAR_FIRST:
        for across in FAR_FIRST:
            for other in range(2):
                if along or across or other:
                    greet(*in_plane(16 * ((core + other) % 2) + 4 * ((y + across) % 4) + (x + along) % 4))
    load_vir.start()
    load_ao.start()
    load_naf.start()

    def vir_copy(other):
        return pltpu.make_async_remote_copy(
            src_ref=vsend, dst_ref=coeffs.at[core, chip],
            send_sem=vir_send, recv_sem=vir_recv,
            device_id=in_plane(16 * core + other), device_id_type=MESH,
        )

    pass_copy = pltpu.make_async_remote_copy(
        src_ref=coeffs.at[core], dst_ref=coeffs.at[core],
        send_sem=pass_send, recv_sem=pass_recv,
        device_id=(r + 1 - 2 * core, c), device_id_type=MESH,
    )

    def raw_copy(dest, turn):
        first, last = SPANS[turn]
        return pltpu.make_async_remote_copy(
            src_ref=stage.at[dest, first:last], dst_ref=raw.at[place, first:last],
            send_sem=raw_send.at[turn], recv_sem=raw_recv.at[turn],
            device_id=in_plane(dest), device_id_type=MESH,
        )

    def term_copy(other):
        return pltpu.make_async_remote_copy(
            src_ref=part.at[other], dst_ref=terms.at[z],
            send_sem=term_send, recv_sem=term_recv,
            device_id=in_line(other), device_id_type=MESH,
        )

    def row_copy(other):
        return pltpu.make_async_remote_copy(
            src_ref=unit, dst_ref=rowp.at[spot],
            send_sem=row_send, recv_sem=row_recv.at[y],
            device_id=(r, other), device_id_type=MESH,
        )

    goal = r // 4
    holds = x // 2 == zl % 2
    at_home = zl == goal
    goal_y = r % 4

    def hold_copy(half):
        return pltpu.make_async_remote_copy(
            src_ref=unit, dst_ref=held.at[zl],
            send_sem=hold_send, recv_sem=hold_recv,
            device_id=(8 * half + i, 4 * goal + y), device_id_type=MESH,
        )

    col_span = pl.ds(4 * y, 4)

    def col_here(other):
        return jnp.logical_and(other == x, jnp.logical_and(goal_y == y, core == y // 2))

    def col_copy(other):
        return pltpu.make_async_remote_copy(
            src_ref=held, dst_ref=colp.at[col_span],
            send_sem=col_send, recv_sem=col_recv,
            device_id=(8 * zh + 2 * other + y // 2, 4 * zl + goal_y), device_id_type=MESH,
        )

    half_span = pl.ds(8 * core, 8)
    half_copy = pltpu.make_async_remote_copy(
        src_ref=colp.at[half_span], dst_ref=colp.at[half_span],
        send_sem=half_send, recv_sem=half_recv,
        device_id=(r + 1 - 2 * core, c), device_id_type=MESH,
    )

    def pair_copy(half):
        return pltpu.make_async_remote_copy(
            src_ref=proj.at[1 - core, half], dst_ref=pair.at[half],
            send_sem=pair_send.at[half], recv_sem=pair_recv.at[half],
            device_id=(r + 1 - 2 * core, c), device_id_type=MESH,
        )

    def proj_copy(half, other, sent):
        if sent:
            pltpu.make_async_remote_copy(
                src_ref=sums.at[half, other], dst_ref=projs.at[4 * zh + x],
                send_sem=proj_send, recv_sem=proj_recv,
                device_id=(8 * half + 2 * other + core, c), device_id_type=MESH,
            ).start()

    def wait_bytes(ref, sem):
        pltpu.make_async_copy(ref, ref, sem).wait()

    load_vir.wait()
    tail = vir[16:20, :].astype(F32)
    vsend[0:16, :] = vir[0:16, :]
    vsend[16:24, :] = jnp.concatenate([tail, tail], axis=0).astype(BF16)
    coeffs[core, chip, :, :] = vsend[...]
    load_ao.wait()
    turns = []
    for quarter in range(4):
        ahead = (quarter + 4 - z // 2) % 4
        turns.append(jnp.where(ahead == 0, 3, jnp.where(ahead == 1, 1, jnp.where(ahead == 2, 0, 2))))
    for dest in range(PLANE):
        tails = []
        for quarter in range(4):
            panel = 8 * (quarter // 2) + 2 * (dest % 4) + dest // 16
            start = 960 * panel + 256 * ((dest // 4) % 4) + 128 * (quarter % 2)
            if start % 128 == 0:
                tile = ao[:, start : start + 128].astype(F32)
            else:
                after = min(start + 64, 15360 - 128)
                tile = jnp.concatenate([ao[:, start : start + 64], ao[:, after : after + 64]], axis=1).astype(F32)
            stage[dest, pl.ds(pl.multiple_of(16 + 16 * turns[quarter], 16), 16), :] = tile[0:16].astype(BF16)
            tails.append(tile[16:20])
        stage[dest, 0:16, :] = jnp.concatenate(tails, axis=0).astype(BF16)
    raw[place, :, :] = stage[place, :, :]

    pl.semaphore_wait(barrier, PLANE - 1 + 2)

    def tell(turn, step):
        pl.semaphore_signal(meet.at[turn], inc=1, device_id=in_line((z + step) % LINE), device_id_type=MESH)

    tell(0, 1)
    tell(0, 7)

    for along in FAR_FIRST:
        for across in FAR_FIRST:
            if along or across:
                vir_copy(4 * ((y + across) % 4) + (x + along) % 4).start()

    for turn in range(len(SPANS)):

        for along in FAR_FIRST:
            for across in FAR_FIRST:
                for other in range(2):
                    if along or across or other:
                        raw_copy(16 * ((core + other) % 2) + 4 * ((y + across) % 4) + (x + along) % 4, turn).start()

    pl.semaphore_wait(meet.at[0], 2)
    tell(1, 2)
    tell(1, 6)
    wait_bytes(coeffs.at[core, pl.ds(0, 15)], vir_recv)
    pass_copy.start()
    pass_copy.wait_recv()

    coeff = coeffs[:, :, 0:16, :].reshape(512, 128).T
    coeff_tail = coeffs[:, :, 16:24, :].astype(F32)
    coeff_tail = jnp.concatenate([coeff_tail, coeff_tail], axis=2).reshape(512, 128).T
    which = (lax.broadcasted_iota(jnp.int32, (128, 512), 1) // 4) % 4
    for turn in range(4):
        quarter = (z // 2 + SHIFTS[turn]) % 4
        first, last = SPANS[turn]
        wait_bytes(raw.at[pl.ds(0, PLANE - 1), first:last], raw_recv.at[turn])
        ints = raw[:, 16 * turn + 16 : 16 * turn + 32, :].reshape(512, 128)
        ints_tail = raw[:, 0:16, :].reshape(512, 128)
        picked = jnp.where(which == quarter, coeff_tail, 0.0).astype(BF16)
        half = jnp.dot(coeff, ints, preferred_element_type=F32) + jnp.dot(picked, ints_tail, preferred_element_type=F32)
        half = half.T
        if turn == 0:
            pl.semaphore_wait(meet.at[1], 2)
        for which_half in range(2):
            other = 2 * quarter + which_half
            part[other, :, :] = half[UNIT * which_half : UNIT * (which_half + 1), :]
            if turn < 3:
                term_copy(other).start()
            else:

                @pl.when(other != z)
                def _():
                    term_copy(other).start()

    terms[z, :, :] = part[z, :, :]
    wait_bytes(terms.at[pl.ds(0, LINE - 1)], term_recv)
    total = terms[0, :, :]
    for s in range(1, LINE):
        total = total + terms[s, :, :]
    unit[...] = total.astype(BF16)

    @pl.when(owns)
    def _():
        pltpu.make_async_copy(unit, rowp.at[spot], row_recv.at[y]).start()

        for across in FAR_FIRST:
            for along in FAR_FIRST:
                if along or across:
                    row_copy(4 * ((zl + along) % 4) + (y + across) % 4).start()

    for half in range(2):

        @pl.when(jnp.logical_and(at_home, zh == half))
        def _():
            pltpu.make_async_copy(unit, held.at[zl], hold_recv).start()

        @pl.when(jnp.logical_not(jnp.logical_and(at_home, zh == half)))
        def _():
            hold_copy(half).start()

    load_naf.wait()
    for group in range(4):
        have = slice(4 * group, min(4 * group + 4, PANEL))
        wait_bytes(rowp.at[have], row_recv.at[group])
    rows = rowp[...].reshape(PANEL * UNIT, 128)
    share = lax.dot_general(rows, naf[...], (((0,), (1,)), ((), ())), preferred_element_type=F32)
    for other in range(16):
        proj[other % 2, other // 8, (other // 2) % 4, :, :] = share[8 * other : 8 * other + 8, :]
    pair_copy(1 - zh).start()
    pair_copy(zh).start()
    @pl.when(holds)
    def _():
        wait_bytes(held, hold_recv)

        @pl.loop(0, 4)
        def _(step):
            other = (x + 2 + 3 * step) % 4

            @pl.when(col_here(other))
            def _():
                pltpu.make_async_copy(held, colp.at[col_span], col_recv).start()

            @pl.when(jnp.logical_not(col_here(other)))
            def _():
                col_copy(other).start()

    for half in (1 - zh, zh):
        pair_copy(half).wait_recv()
        sums[half, :, :, :] = proj[core, half] + pair[half]
        for step in FAR_FIRST:
            proj_copy(half, (x + step) % 4, half is not zh or step != 0)
    projs[4 * zh + x, :, :] = sums[zh, x]

    wait_bytes(colp.at[half_span], col_recv)
    half_copy.start()
    half_copy.wait_recv()
    wait_bytes(coeffs.at[core, pl.ds(0, 15)], vir_send)
    pass_copy.wait_send()
    for turn in range(len(SPANS)):
        first, last = SPANS[turn]
        wait_bytes(stage.at[pl.ds(0, PLANE - 1), first:last], raw_send.at[turn])
    wait_bytes(part.at[pl.ds(0, LINE - 1)], term_send)

    @pl.when(owns)
    def _():
        wait_bytes(rowp, row_send)

    for count in range(1, 3):

        @pl.when(jnp.where(at_home, 1, 2) == count)
        def _():
            wait_bytes(held.at[0:count], hold_send)

    for count in range(3, 5):

        @pl.when(jnp.logical_and(holds, jnp.where(col_here(x), 3, 4) == count))
        def _():
            wait_bytes(terms.at[0 : 2 * count], col_send)

    half_copy.wait_send()
    for half in range(2):
        pair_copy(half).wait_send()
    wait_bytes(projs.at[pl.ds(0, 7)], proj_recv)
    total = projs[0, :, :]
    for s in range(1, 8):
        total = total + projs[s, :, :]
    naf_ref[...] = total

    wait_bytes(projs.at[pl.ds(0, 7)], proj_send)


BANDS = 5


def finish(rowp, colp, naf_ref, gram_hbm, naf_hbm, gram, sems):
    pltpu.make_async_copy(naf_ref, naf_hbm, sems.at[BANDS]).start()
    cols = colp[0:PANEL, :, :].reshape(PANEL * UNIT, 128)
    rows = PANEL * UNIT // BANDS
    copies = []
    for band in range(BANDS):
        block = rowp[3 * band : 3 * band + 3, :, :].reshape(rows, 128)
        gram[rows * band : rows * (band + 1), :] = contract_second(block, cols) * (1.0 / 128)
        span = pl.ds(rows * band, rows)
        copies.append(pltpu.make_async_copy(gram.at[span], gram_hbm.at[span], sems.at[band]))
        copies[-1].start()
    for copy in copies:
        copy.wait()
    pltpu.make_async_copy(naf_ref, naf_hbm, sems.at[BANDS]).wait()


def shards(ao_ints, vir_coef, naf_vectors):
    dma = pltpu.SemaphoreType.DMA
    hbm = pl.BlockSpec(memory_space=pltpu.HBM)
    rowp, colp, naf_ints = pl.pallas_call(
        kernel,
        out_shape=(
            jax.ShapeDtypeStruct((PANEL, UNIT, 128), BF16),
            jax.ShapeDtypeStruct((16, UNIT, 128), BF16),
            jax.ShapeDtypeStruct((8, 448), F32),
        ),
        in_specs=[hbm, hbm, hbm],
        out_specs=[pl.BlockSpec(memory_space=pltpu.VMEM)] * 3,
        scratch_shapes=[
            pltpu.VMEM((20, 15360), BF16),
            pltpu.VMEM((20, 128), BF16),
            pltpu.VMEM((448, 960), BF16),
            pltpu.VMEM((PLANE, 80, 128), BF16),
            pltpu.VMEM((PLANE, 80, 128), BF16),
            pltpu.VMEM((24, 128), BF16),
            pltpu.VMEM((2, 16, 24, 128), BF16),
            pltpu.VMEM((LINE, UNIT, 128), F32),
            pltpu.VMEM((LINE, UNIT, 128), F32),
            pltpu.VMEM((UNIT, 128), BF16),
            pltpu.VMEM((4, UNIT, 128), BF16),
            pltpu.VMEM((2, 2, 4, 8, 448), F32),
            pltpu.VMEM((2, 4, 8, 448), F32),
            pltpu.VMEM((2, 4, 8, 448), F32),
            pltpu.VMEM((8, 8, 448), F32),
            dma((3,)), dma, dma, dma, dma, dma((4,)), dma((4,)), dma, dma,
            dma, dma((4,)), dma, dma, dma, dma, dma, dma, dma((2,)), dma((2,)), dma, dma,
            pltpu.SemaphoreType.REGULAR((2,)),
        ],
        compiler_params=pltpu.CompilerParams(
            collective_id=0, has_side_effects=True, vmem_limit_bytes=40 * 1024 * 1024
        ),
        name="panels_and_projection",
    )(*(pltpu.with_memory_space_constraint(a, pltpu.HBM) for a in (ao_ints, vir_coef, naf_vectors.T)))
    return pl.pallas_call(
        finish,
        out_shape=(
            jax.ShapeDtypeStruct((960, 960), F32),
            jax.ShapeDtypeStruct((8, 448), F32),
        ),
        in_specs=[pl.BlockSpec(memory_space=pltpu.VMEM)] * 3,
        out_specs=(hbm, hbm),
        scratch_shapes=[pltpu.VMEM((960, 960), F32), dma((BANDS + 1,))],
        compiler_params=pltpu.CompilerParams(vmem_limit_bytes=16 * 1024 * 1024),
        name="gram",
    )(rowp, colp, naf_ints)


def solution(mesh):
    in_specs = (P(("row", "col"), None), P(("row", "col"), None), P("row", "col"))
    out_specs = (P("row", "col"), P("row", "col"))
    return jax.shard_map(shards, mesh=mesh, in_specs=in_specs, out_specs=out_specs, check_vma=False)
```
